32 devices in a mesh: seq: 4 (over x, core), grp: 8 (over z, y).
Axes of the slice: x: 2, y: 2, z: 4, core: 2. Of those that a mesh axis runs over, the one named last changes fastest.
Arguments:
- tokens: bfloat16 [8, 512, 1408], P('grp', 'seq'), may hold values from -6 to 6
- target_kv: bfloat16 [1408, 1408], P('seq'), may hold values from -0.15625 to 0.15625
- context_kv: bfloat16 [1408, 1408], P('seq'), may hold values from -0.15625 to 0.15625
- query_weight: bfloat16 [704, 1408], replicated, may hold values from -0.15625 to 0.15625
- pred_hidden: bfloat16 [8, 512, 384], P('grp', 'seq'), may hold values from -6 to 6
- pred_weight: bfloat16 [8, 704, 384], P('grp'), may hold values from -0.3125 to 0.3125
- target_mask: int32 [8, 256], P('grp', 'seq'), may hold values 0 or 1
- owners: int32 [8, 256, 1], P('grp', 'seq'), may hold values from 0 to 7; in each aligned block of 64 rows (0 to 63, 64 to 127, ..., all dimensions but the last counted through in order) at most 8 rows name the same one
Outputs:
- new_kv: bfloat16 [1408, 1408], P('seq')
- targets: bfloat16 [8, 512, 704], P('grp', 'seq')
- pred_grad: bfloat16 [8, 512, 384], P('grp', 'seq')
The draws below stay inside these ranges and needn't reach their ends.
Inputs may be any that keep to these rules, and one draw needn't show every extreme that they name: `owners`: among the 64 token pairs of one device no owner is named more than 8 times, a bound that some block reaches.
All inputs are finite; a program needn't handle non-finite values. No bound on the sum of `target_mask` on one device may be relied on, other than what follows from the above.
Results may differ from the reference program's by a relative error of at most 0.011.
Values may be sent and summed in bfloat16 or wider, within the bound.
No kernel may reach another device: no remote copies, remote signals or barrier semaphores. Data moves between devices by JAX's collectives and lax.ppermute only.
A program may use at most 64 MiB of HBM per device.

```python
import math
import jax
import jax.numpy as jnp
import numpy as np
from jax import lax

D = 1408
HEAD = 64
HEADS = 11
PRED = 384
ATT = 704
CLIP_TOK = 512
CLIPS = 8
BLOCKS_DEV = 64
BLOCKS = 256
CAP = 8
EXPERTS = 8


def plant(entries, own_key, low, top_value):
    longest = entries.shape.index(max(entries.shape))
    spots = []
    for shift in (0, 1):
        where = [jax.random.randint(jax.random.fold_in(own_key, axis), (), 0, length) for axis, length in enumerate(entries.shape)]
        where[longest] = (where[longest] + shift) % entries.shape[longest]
        spots.append(tuple(where))
    return entries.at[spots[0]].set(low).at[spots[1]].set(top_value)


def shard_levels(stream_key, extent, split, least, largest):
    level = 1.0
    for dim, shards_of in split:
        draws = jax.random.uniform(jax.random.fold_in(jax.random.fold_in(stream_key, 6), dim), (shards_of,), jnp.float32, least / len(split), largest / len(split))
        level = level * jnp.repeat(jnp.exp(draws), extent[dim] // shards_of).reshape((-1,) + (1,) * (len(extent) - 1 - dim))
    return level


def shared_out(stream_key, own, number, rows, amount, top, reach, skew):
    ranking = jax.random.permutation(stream_key, amount)
    packed, usual = load_shares(amount, rows * top, reach, skew, True), load_shares(amount, rows * top, reach, skew, False)
    places = jnp.arange(amount)

    def named(tallies, offset_by):
        used = int((tallies > 0).sum())
        fixed = max(1, used // 4)
        passed = fixed + (places - fixed + offset_by * (used - fixed)) % max(1, amount - fixed)
        return jnp.zeros((amount,), jnp.int32).at[ranking[jnp.where(places < fixed, places, passed)]].set(jnp.asarray(tallies, jnp.int32))

    tallies = jnp.where(number % 4 == 0, named(packed, number // 4), named(usual, number - number // 4 - 1))
    mixed = jax.random.permutation(jax.random.fold_in(own, 3), amount)
    donor, receiver = mixed[0:amount // 2 * 2:2], mixed[1:amount // 2 * 2:2]
    room = jnp.minimum(tallies[donor] - 1, reach - tallies[receiver]) // 2
    room = jnp.where((donor == ranking[0]) | (receiver == ranking[0]) | (tallies[receiver] == 0), 0, jnp.maximum(room, 0))
    passed = jax.random.randint(jax.random.fold_in(own, 4), (amount // 2,), 0, 1 << 20) % (room + 1)
    tallies = tallies.at[donor].add(-passed).at[receiver].add(passed)
    items = jnp.searchsorted(jnp.cumsum(tallies), jnp.arange(rows * top), side="right").astype(jnp.int32)
    table = items.reshape(top, rows).T
    table = table[jax.random.permutation(jax.random.fold_in(own, 1), rows)]
    offset_by = jax.random.randint(jax.random.fold_in(own, 2), (rows, 1), 0, top)
    return jnp.take_along_axis(table, (jnp.arange(top)[None, :] + offset_by) % top, axis=1)


def load_shares(number_of, total, reach, lean, full):
    weights = [(1 << 20) // math.isqrt(grade ** lean) + 1 for grade in range(1, number_of + 1)]
    largest = reach if full else min(reach, max(-(-total // number_of), total * weights[0] // sum(weights)))
    least = 1 if total - largest >= number_of - 1 else 0
    given, spare = [largest] + [least] * (number_of - 1), total - largest - least * (number_of - 1)
    while spare > 0:
        candidates = [i for i in range(1, number_of) if given[i] < largest] or [i for i in range(1, number_of) if given[i] < reach]
        whole, remaining = sum([weights[i] for i in candidates]), spare
        for i in candidates:
            extra = min(reach - given[i], max(1, remaining * weights[i] // whole), spare)
            given[i] = given[i] + extra
            spare = spare - extra
    return np.array(given)


def centred(rng, dims, scale, reach, shards=(), kind=jnp.bfloat16):
    array = jax.random.normal(rng, dims, jnp.float32) * scale
    if len(shards) > 0:
        array = shard_levels(rng, dims, shards, -0.22, 0.18) * array
    return jnp.clip(array, min=-reach, max=reach).astype(kind)


def setup_inputs(seed: int = 0) -> dict:
    key_of = jax.random.split(jax.random.key(seed), 9)
    tokens = centred(key_of[0], (CLIPS, CLIP_TOK, D), 1.0, 6.0, ((0, 8), (1, 4)))
    target_kv = centred(key_of[1], (D, 2 * ATT), D ** -0.5, 0.15625, ((0, 4),))
    context_kv = centred(key_of[2], (D, 2 * ATT), D ** -0.5, 0.15625, ((0, 4),))
    query_weight = centred(key_of[3], (ATT, D), D ** -0.5, 0.15625)
    pred_hidden = centred(key_of[4], (CLIPS, CLIP_TOK, PRED), 1.0, 6.0, ((0, 8), (1, 4)))
    pred_weight = centred(key_of[5], (EXPERTS, ATT, PRED), PRED ** -0.5, 0.3125, ((0, 8),))
    target_mask = plant((jax.random.randint(key_of[6], (CLIPS, BLOCKS), 0, 4) < 3).astype(jnp.int32), jax.random.fold_in(key_of[6], 1), 0, 1)
    owners_keys = jax.random.split(jax.random.fold_in(key_of[7], 1), CLIPS * BLOCKS // BLOCKS_DEV)
    owners_turns = jax.random.permutation(jax.random.fold_in(key_of[7], 3), CLIPS * BLOCKS // BLOCKS_DEV)
    owners = jax.vmap(lambda own, number: shared_out(jax.random.fold_in(key_of[7], 2), own, number, BLOCKS_DEV, EXPERTS, 1, CAP, 2))(owners_keys, owners_turns).reshape((CLIPS, BLOCKS, 1))
    return {"tokens": tokens, "target_kv": target_kv, "context_kv": context_kv, "query_weight": query_weight, "pred_hidden": pred_hidden, "pred_weight": pred_weight, "target_mask": target_mask, "owners": owners}


keep_rate = 0.9
epsilon = 1e-05

def layer_norm(values):
    center = values - lax.optimization_barrier(jnp.mean(values, axis=-1, keepdims=True))
    variance = lax.optimization_barrier(jnp.mean(center * center, axis=-1, keepdims=True))
    return center * lax.rsqrt(variance + epsilon)

def rounded(values):
    return lax.optimization_barrier(values.astype(jnp.bfloat16)).astype(jnp.float32)

def norm_backward(upstream, normed, inputs):
    center = inputs - lax.optimization_barrier(jnp.mean(inputs, axis=-1, keepdims=True))
    variance = lax.optimization_barrier(jnp.mean(center * center, axis=-1, keepdims=True))
    inverse = lax.rsqrt(variance + epsilon)
    upstream_mean = lax.optimization_barrier(jnp.mean(upstream, axis=-1, keepdims=True))
    cross_mean = lax.optimization_barrier(jnp.mean(upstream * normed, axis=-1, keepdims=True))
    return inverse * (upstream - upstream_mean - normed * cross_mean)

def reference(tokens, target_kv, context_kv, query_weight, pred_hidden, pred_weight, target_mask, owners):
    blended = (keep_rate * target_kv.astype(jnp.float32) + (1.0 - keep_rate) * context_kv.astype(jnp.float32)).astype(jnp.bfloat16)
    width = HEADS * HEAD
    scale = 1.0 / math.sqrt(HEAD)

    def clip_targets(clip):
        length = clip.shape[0]
        normed = layer_norm(clip.astype(jnp.float32)).astype(jnp.bfloat16)
        queries = rounded(jnp.dot(normed, query_weight.T, preferred_element_type=jnp.float32))
        key_values = rounded(jnp.dot(normed, blended, preferred_element_type=jnp.float32))
        query_heads = queries.reshape(length, HEADS, HEAD)
        keys = key_values[:, :width].reshape(length, HEADS, HEAD)
        values = key_values[:, width:].reshape(length, HEADS, HEAD)
        scores = jnp.einsum('qhd,khd->hqk', query_heads, keys) * scale
        expo = jnp.exp(scores)
        denominator = lax.optimization_barrier(jnp.sum(expo, axis=-1))
        numerator = jnp.einsum('hqk,khd->qhd', rounded(expo), values)
        attended = (numerator / denominator.T[:, :, None]).reshape(length, width)
        return layer_norm(attended).astype(jnp.bfloat16)
    targets = lax.map(clip_targets, tokens)
    pred_size = pred_hidden.shape[2]
    flat_hidden = pred_hidden.reshape(-1, pred_size)
    flat_targets = targets.reshape(-1, width)
    owner_tokens = jnp.repeat(owners[:, :, 0], 2, axis=1).reshape(-1).astype(jnp.int32)
    live_tokens = jnp.repeat(target_mask, 2, axis=1).reshape(-1)
    total = flat_hidden.shape[0]
    block = math.gcd(total, 256)
    count = total // block

    def block_grad(pieces):
        hidden, target_rows, owner_ids, live = pieces
        inputs = hidden.astype(jnp.float32)
        normed = layer_norm(inputs)
        experts = pred_weight[owner_ids].astype(jnp.float32)
        prediction = jnp.einsum('tp,tap->ta', rounded(normed), experts)
        residual = prediction - target_rows.astype(jnp.float32)
        upstream = jnp.einsum('ta,tap->tp', rounded(residual), experts)
        grad = norm_backward(upstream, normed, inputs)
        return (grad * live[:, None].astype(jnp.float32)).astype(jnp.bfloat16)
    grads = lax.map(block_grad, (flat_hidden.reshape(count, block, pred_size), flat_targets.reshape(count, block, width), owner_tokens.reshape(count, block), live_tokens.reshape(count, block)))
    return (blended, targets, grads.reshape(pred_hidden.shape))
```

```python
import math

import jax
import jax.numpy as jnp
from jax import lax
from jax.experimental import pallas as pl
from jax.experimental.pallas import tpu as pltpu
from jax.sharding import PartitionSpec as P

HEAD = 64
HEADS = 11


keep_rate = 0.9
epsilon = 1e-05


def layer_norm(values):
    center = values - jnp.mean(values, axis=-1, keepdims=True)
    variance = jnp.mean(center * center, axis=-1, keepdims=True)
    return center * lax.rsqrt(variance + epsilon)


def norm_backward(upstream, normed, inputs):
    center = inputs - jnp.mean(inputs, axis=-1, keepdims=True)
    variance = jnp.mean(center * center, axis=-1, keepdims=True)
    inverse = lax.rsqrt(variance + epsilon)
    upstream_mean = jnp.mean(upstream, axis=-1, keepdims=True)
    cross_mean = jnp.mean(upstream * normed, axis=-1, keepdims=True)
    return inverse * (upstream - upstream_mean - normed * cross_mean)


def owner_compute(received, expert_weight):
    received_targets, received_hidden = received
    groups = received_targets.shape[0]
    items = received_targets.shape[1]
    pred_size = expert_weight.shape[1]
    width = expert_weight.shape[0]
    inputs = received_hidden.reshape(-1, pred_size).astype(jnp.float32)
    normed = layer_norm(inputs)
    prediction = jnp.einsum(
        "tp,ap->ta", normed.astype(jnp.bfloat16), expert_weight, preferred_element_type=jnp.float32
    )
    residual = prediction - received_targets.reshape(-1, width).astype(jnp.float32)
    upstream = jnp.dot(
        residual.astype(jnp.bfloat16), expert_weight, preferred_element_type=jnp.float32
    )
    grad = norm_backward(upstream, normed, inputs).astype(jnp.bfloat16)
    return grad.reshape(groups, items, 2 * pred_size)


def general_shards(
    tokens, target_kv, context_kv, query_weight, pred_hidden, pred_weight, target_mask, owners
):
    new_kv = (
        keep_rate * target_kv.astype(jnp.float32)
        + (1.0 - keep_rate) * context_kv.astype(jnp.float32)
    ).astype(jnp.bfloat16)
    width = HEADS * HEAD
    scale = 1.0 / math.sqrt(HEAD)
    rows = tokens.shape[1]
    normed = layer_norm(tokens[0].astype(jnp.float32)).astype(jnp.bfloat16)
    queries = jnp.einsum(
        "td,ad->ta", normed, query_weight, preferred_element_type=jnp.float32
    ).astype(jnp.bfloat16)
    query_heads = queries.reshape(rows, HEADS, HEAD)
    own_kv = jnp.dot(
        normed,
        lax.all_gather(new_kv, "seq", axis=0, tiled=True),
        preferred_element_type=jnp.float32,
    ).astype(jnp.bfloat16)
    key_values = lax.all_gather(own_kv, "seq", axis=0, tiled=True)
    count = key_values.shape[0]
    keys = key_values[:, :width].reshape(count, HEADS, HEAD)
    values = key_values[:, width:].reshape(count, HEADS, HEAD)
    scores = (
        jnp.einsum("qhd,khd->hqk", query_heads, keys, preferred_element_type=jnp.float32) * scale
    )
    expo = jnp.exp(scores)
    added = jnp.einsum(
        "hqk,khd->qhd", expo.astype(jnp.bfloat16), values, preferred_element_type=jnp.float32
    )
    numerator = added.reshape(rows, width)
    denominator = jnp.sum(expo, axis=-1)
    attended = (numerator.reshape(rows, HEADS, HEAD) / denominator.T[:, :, None]).reshape(
        rows, width
    )
    targets = layer_norm(attended).astype(jnp.bfloat16)
    blocks = target_mask.shape[1]
    groups = lax.axis_size("grp")
    capacity = max(2, (blocks + groups - 1) // groups)
    pred_size = pred_hidden.shape[2]
    owner_ids = owners[0, :, 0]
    live = target_mask[0]
    chosen = (
        (owner_ids[:, None] == jnp.arange(groups, dtype=jnp.int32)[None, :]) & (live[:, None] == 1)
    ).astype(jnp.int32)
    earlier = jnp.cumsum(chosen, axis=0) - chosen
    position = jnp.sum(earlier * chosen, axis=1)
    slot_index = owner_ids * capacity + position
    dispatch = (
        (jnp.arange(groups * capacity, dtype=jnp.int32)[:, None] == slot_index[None, :])
        & (live[None, :] == 1)
    ).astype(jnp.bfloat16)
    send_targets = (
        jnp.dot(dispatch, targets.reshape(blocks, 2 * width), preferred_element_type=jnp.float32)
        .astype(jnp.bfloat16)
        .reshape(groups, capacity, 2 * width)
    )
    send_hidden = (
        jnp.dot(
            dispatch,
            pred_hidden[0].reshape(blocks, 2 * pred_size),
            preferred_element_type=jnp.float32,
        )
        .astype(jnp.bfloat16)
        .reshape(groups, capacity, 2 * pred_size)
    )
    expert_weight = pred_weight[0]
    owner_grads = owner_compute(
        (
            lax.all_to_all(send_targets, "grp", split_axis=0, concat_axis=0, tiled=True),
            lax.all_to_all(send_hidden, "grp", split_axis=0, concat_axis=0, tiled=True),
        ),
        expert_weight,
    )
    back_grads = lax.all_to_all(owner_grads, "grp", split_axis=0, concat_axis=0, tiled=True)
    pair_grads = jnp.dot(
        dispatch.T,
        back_grads.reshape(groups * capacity, 2 * pred_size),
        preferred_element_type=jnp.float32,
    )
    pred_grad = pair_grads.astype(jnp.bfloat16).reshape(rows, pred_size)
    return (new_kv, targets[None], pred_grad[None])


LANES = 128
PAIR_BUDGET = 16 << 20
VM = pl.BlockSpec(memory_space=pltpu.VMEM)
SM = pl.BlockSpec(memory_space=pltpu.SMEM)


def vmem_call(body, outs, operands, specs=None, cost=None, scratch=()):
    return pl.pallas_call(
        body,
        out_shape=outs,
        in_specs=specs or [VM] * len(operands),
        out_specs=jax.tree.map(lambda _: VM, outs),
        scratch_shapes=list(scratch),
        cost_estimate=cost,
    )(*operands)


def shape_of(dims, kind=jnp.bfloat16):
    return jax.ShapeDtypeStruct(dims, kind)


def matmul_cost(rows, depth, columns, extra=0):
    return pl.CostEstimate(
        flops=2 * rows * depth * columns, bytes_accessed=2 * depth * columns, transcendentals=extra
    )


def chip_tiles(tiles, is_first, offset):
    lane = lax.broadcasted_iota(jnp.int32, tiles[0].shape, 1) < HEAD
    half = len(tiles) // 2 if offset else len(tiles)
    mixed = jnp.where(lane, tiles[5], tiles[2])
    first = [tiles[0], tiles[1], tiles[2]]
    second = [tiles[3], tiles[4], mixed]
    if offset:
        first = first + tiles[5:8]
        second = second + tiles[8:11]
    own = [jnp.where(is_first, a, b) for a, b in zip(first, second)]
    other = [jnp.where(is_first, b, a) for a, b in zip(first, second)]
    return own, other


def norm_body(place, tokens, normed, keep, send):
    half = tokens.shape[1] // 2
    values = layer_norm(tokens[...].astype(jnp.float32)).astype(jnp.bfloat16)
    normed[...] = values
    low, high = values[:, :half], values[:, half:]
    is_first = place[0] == 0
    keep[...] = jnp.where(is_first, low, high)
    send[...] = jnp.where(is_first, high, low)


def query_body(place, normed, weight, own, other):
    queries = lax.dot_general(
        normed[...], weight[...], (((1,), (1,)), ((), ())), preferred_element_type=jnp.float32
    ).astype(jnp.bfloat16).astype(jnp.float32) * (1.0 / math.sqrt(HEAD))
    full = queries.shape[1] // LANES
    tiles = [queries[:, t * LANES : (t + 1) * LANES] for t in range(full)]
    rest = queries[:, full * LANES :]
    tiles.append(jnp.concatenate([rest, jnp.zeros_like(rest)], axis=1))
    mine, theirs = chip_tiles(tiles, place[0] == 0, False)
    for t in range(3):
        own[:, t * LANES : (t + 1) * LANES] = mine[t].astype(jnp.bfloat16)
        other[:, t * LANES : (t + 1) * LANES] = theirs[t].astype(jnp.bfloat16)


def weight_body(place, own, other, joined):
    rows = own.shape[0]
    core = place[1]
    joined[pl.ds(pl.multiple_of(core * rows, 16), rows), :] = own[...]
    joined[pl.ds(pl.multiple_of((1 - core) * rows, 16), rows), :] = other[...]


def partial_body(place, rows, weight, own, other):
    sums = jnp.dot(rows[...], weight[...], preferred_element_type=jnp.float32)
    tiles = [sums[:, t * LANES : (t + 1) * LANES] for t in range(sums.shape[1] // LANES)]
    mine, theirs = chip_tiles(tiles, place[0] == 0, True)
    for t in range(6):
        own[:, t * LANES : (t + 1) * LANES] = mine[t]
        other[:, t * LANES : (t + 1) * LANES] = theirs[t].astype(jnp.bfloat16)


def attend_body(q_own, q_other, kv_a, kv_b, mine, theirs):
    rows = q_own.shape[0]
    count = 6
    for queries, out in ((q_own, mine), (q_other, theirs)):
        found = [None] * count
        for slot in range(count):
            tile, upper = slot // 2, slot % 2
            lane = lax.broadcasted_iota(jnp.int32, (1, LANES), 1) >= HEAD
            lane = lane if upper else jnp.logical_not(lane)
            q = queries[:, tile * LANES : (tile + 1) * LANES]
            q = jnp.where(lane, q, jnp.zeros_like(q))
            to = (slot + 1) % count
            v_tile, v_upper = to // 2, to % 2
            v_lane = lax.broadcasted_iota(jnp.int32, (1, LANES), 1) >= HEAD
            v_lane = v_lane if v_upper else jnp.logical_not(v_lane)
            total = None
            for kv in (kv_a, kv_b):
                keys = kv[:, tile * LANES : (tile + 1) * LANES]
                scores = lax.dot_general(
                    q, keys, (((1,), (1,)), ((), ())), preferred_element_type=jnp.float32
                )
                weights = jnp.exp(scores).astype(jnp.bfloat16)
                start = (3 + v_tile) * LANES
                values = kv[:, start : start + LANES]
                values = jnp.where(v_lane, values, jnp.ones_like(values))
                part = jnp.dot(weights, values, preferred_element_type=jnp.float32)
                total = part if total is None else total + part
            found[to] = total / pltpu.roll(total, HEAD, 1)
        for t in range(3):
            lane = lax.broadcasted_iota(jnp.int32, (1, LANES), 1) < HEAD
            joined = jnp.where(lane, found[2 * t], found[2 * t + 1])
            out[:, t * LANES : (t + 1) * LANES] = joined.astype(out.dtype)


def predict_body(place, slots, owner, hidden, own_weight, *refs):
    pieces = refs[: len(refs) // 2 - 1]
    swapped = refs[len(refs) // 2 - 1 : -2]
    prediction, weights = refs[-2], refs[-1]
    core = place[1]
    rows = pieces[0].shape[0]
    low = pl.multiple_of(core * rows, 16)
    high = pl.multiple_of((1 - core) * rows, 16)
    weights[0] = own_weight[...]
    for slot, (mine, theirs) in enumerate(zip(pieces, swapped)):
        weights[slot + 1, pl.ds(low, rows), :] = mine[...]
        weights[slot + 1, pl.ds(high, rows), :] = theirs[...]
    normed = layer_norm(hidden[...].astype(jnp.float32)).astype(jnp.bfloat16)
    ids = owner[...]
    total = jnp.zeros(prediction.shape, jnp.float32)
    for slot in range(len(pieces) + 1):
        picked = jnp.where(ids == slots[slot], normed, jnp.zeros_like(normed))
        total = total + lax.dot_general(
            picked, weights[slot], (((1,), (1,)), ((), ())), preferred_element_type=jnp.float32
        )
    prediction[...] = total


def finish_body(
    place, slots, owner, live, attended, returned, prediction, hidden, weights, targets, grad
):
    width = targets.shape[1]
    is_first = place[0] == 0
    mine, theirs = attended[...], returned[...].astype(jnp.float32)
    joined = jnp.concatenate(
        [jnp.where(is_first, mine, theirs), jnp.where(is_first, theirs, mine)], axis=1
    )
    lane = lax.broadcasted_iota(jnp.int32, joined.shape, 1) >= HEAD
    joined = jnp.where(lane, joined, 0.0)
    mean = jnp.sum(joined, axis=1, keepdims=True) * (1.0 / width)
    center = jnp.where(lane, joined - mean, 0.0)
    variance = jnp.sum(center * center, axis=1, keepdims=True) * (1.0 / width)
    found = (center * lax.rsqrt(variance + epsilon))[:, HEAD:].astype(jnp.bfloat16)
    targets[...] = found
    residual = (prediction[...] - found.astype(jnp.float32)).astype(jnp.bfloat16)
    ids = owner[...]
    upstream = jnp.zeros(hidden.shape, jnp.float32)
    for slot in range(weights.shape[0]):
        picked = jnp.where(ids == slots[slot], residual, jnp.zeros_like(residual))
        upstream = upstream + jnp.dot(picked, weights[slot], preferred_element_type=jnp.float32)
    inputs = hidden[...].astype(jnp.float32)
    back = norm_backward(upstream, layer_norm(inputs), inputs)
    grad[...] = jnp.where(live[...] == 1, back, 0.0).astype(grad.dtype)


def gather_ring(piece, groups):
    order = list(range(0, groups, 2)) + list(range(groups - 1, 0, -2))
    ahead = [(order[i], order[(i + 1) % groups]) for i in range(groups)]
    behind = [(b, a) for a, b in ahead]
    forward, backward = [], []
    for table, found, steps in ((ahead, forward, groups // 2), (behind, backward, (groups - 1) // 2)):
        held = piece
        for _ in range(steps):
            held = lax.ppermute(held, "grp", table)
            found.append(held)
    where = {g: i for i, g in enumerate(order)}
    slots = [
        [g]
        + [order[(where[g] - k - 1) % groups] for k in range(len(forward))]
        + [order[(where[g] + k + 1) % groups] for k in range(len(backward))]
        for g in range(groups)
    ]
    return forward + backward, jnp.array(slots, jnp.int32)


def paired_shards(
    tokens, target_kv, context_kv, query_weight, pred_hidden, pred_weight, target_mask, owners
):
    members = lax.axis_size("seq")
    groups = lax.axis_size("grp")
    across = [(i, (i + members // 2) % members) for i in range(members)]
    beside = [(i, i ^ 1) for i in range(members)]
    me = lax.axis_index("seq")
    chip, core = me // 2, me % 2
    place = jnp.stack([chip, core]).astype(jnp.int32)
    rows, width = tokens.shape[1], query_weight.shape[0]
    features = tokens.shape[2]
    half = features // 2
    packed = 3 * LANES
    pred_size = pred_hidden.shape[2]

    half_rows = pred_weight.shape[1] // 2
    piece = lax.dynamic_slice(
        pred_weight[0], (core * half_rows, 0), (half_rows, pred_size)
    )

    normed, keep, send = vmem_call(
        norm_body,
        [shape_of((rows, features)), shape_of((rows, half)), shape_of((rows, half))],
        (place, tokens[0]),
        [SM, VM],
    )
    kept_other = lax.ppermute(send, "seq", across)
    new_kv = (
        keep_rate * target_kv.astype(jnp.float32)
        + (1.0 - keep_rate) * context_kv.astype(jnp.float32)
    ).astype(jnp.bfloat16)
    other_kv = lax.ppermute(new_kv, "seq", beside)
    q_own, q_send = vmem_call(
        query_body,
        [shape_of((rows, packed)), shape_of((rows, packed))],
        (place, normed, query_weight),
        [SM, VM, VM],
        matmul_cost(rows, features, width),
    )
    q_other = lax.ppermute(q_send, "seq", across)
    joined = vmem_call(
        weight_body, shape_of((half, 2 * width)), (place, new_kv, other_kv), [SM, VM, VM]
    )

    def partial(values):
        return vmem_call(
            partial_body,
            [shape_of((rows, 2 * packed), jnp.float32), shape_of((rows, 2 * packed))],
            (place, values, joined),
            [SM, VM, VM],
            matmul_cost(rows, half, 2 * width),
        )

    own_sum, own_send = partial(keep)
    from_own = lax.ppermute(own_send, "seq", across)
    other_sum, other_send = partial(kept_other)
    from_other = lax.ppermute(other_send, "seq", across)
    kv = jnp.concatenate(
        [
            (other_sum + from_own.astype(jnp.float32)).astype(jnp.bfloat16),
            (own_sum + from_other.astype(jnp.float32)).astype(jnp.bfloat16),
        ],
        axis=0,
    )
    kv_beside = lax.ppermute(kv, "seq", beside)
    attended, send_back = vmem_call(
        attend_body,
        [shape_of((rows, packed), jnp.float32), shape_of((rows, packed))],
        (q_own, q_other, kv, kv_beside),
    )
    returned = lax.ppermute(send_back, "seq", across)

    pieces, slot_table = gather_ring(piece, groups)
    swapped = [lax.ppermute(p, "seq", beside) for p in pieces]
    slots = lax.dynamic_index_in_dim(slot_table, lax.axis_index("grp"), 0, keepdims=False)
    owner = jnp.repeat(owners[0, :, 0], 2).reshape(rows, 1)
    live = jnp.repeat(target_mask[0], 2).reshape(rows, 1)
    prediction, weights = vmem_call(
        predict_body,
        [
            shape_of((rows, width), jnp.float32),
            shape_of((groups, width, pred_size)),
        ],
        (place, slots, owner, pred_hidden[0], pred_weight[0], *pieces, *swapped),
        [SM, SM] + [VM] * (3 + 2 * len(pieces)),
        matmul_cost(rows, groups * pred_size, width),
    )
    targets, grad = vmem_call(
        finish_body,
        [shape_of((rows, width)), shape_of((rows, pred_size))],
        (
            place, slots, owner, live, attended, returned, prediction, pred_hidden[0], weights
        ),
        [SM, SM] + [VM] * 7,
        matmul_cost(rows, groups * pred_size, width),
    )
    return (new_kv, targets[None], grad[None])


def shards(*arguments):
    pred_weight = arguments[5]
    gathered = lax.axis_size("grp") * pred_weight.size * pred_weight.dtype.itemsize
    two_chips = lax.axis_size("seq") == 4
    if two_chips and lax.axis_size("grp") % 2 == 0 and gathered <= PAIR_BUDGET:
        return paired_shards(*arguments)
    return general_shards(*arguments)


def solution(mesh):
    placed = (
        P("grp", "seq", None),
        P("seq", None),
        P("seq", None),
        P(),
        P("grp", "seq", None),
        P("grp", None, None),
        P("grp", "seq"),
        P("grp", "seq", None),
    )
    return jax.shard_map(
        shards,
        mesh=mesh,
        in_specs=placed,
        out_specs=(P("seq", None), P("grp", "seq", None), P("grp", "seq", None)),
        check_vma=False,
    )
```

```python
import functools
import math

import jax
import jax.numpy as jnp
from jax import lax
from jax.experimental import pallas as pl
from jax.experimental.pallas import tpu as pltpu
from jax.sharding import PartitionSpec as P


HEAD = 64
HEADS = 11


keep_rate = 0.9
epsilon = 1e-05


def layer_norm(values):
    center = values - jnp.mean(values, axis=-1, keepdims=True)
    variance = jnp.mean(center * center, axis=-1, keepdims=True)
    return center * lax.rsqrt(variance + epsilon)


def norm_backward(upstream, normed, inputs):
    center = inputs - jnp.mean(inputs, axis=-1, keepdims=True)
    variance = jnp.mean(center * center, axis=-1, keepdims=True)
    inverse = lax.rsqrt(variance + epsilon)
    upstream_mean = jnp.mean(upstream, axis=-1, keepdims=True)
    cross_mean = jnp.mean(upstream * normed, axis=-1, keepdims=True)
    return inverse * (upstream - upstream_mean - normed * cross_mean)


def owner_compute(received, expert_weight):
    received_targets, received_hidden = received
    groups = received_targets.shape[0]
    items = received_targets.shape[1]
    pred_size = expert_weight.shape[1]
    width = expert_weight.shape[0]
    inputs = received_hidden.reshape(-1, pred_size).astype(jnp.float32)
    normed = layer_norm(inputs)
    prediction = jnp.einsum(
        "tp,ap->ta", normed.astype(jnp.bfloat16), expert_weight, preferred_element_type=jnp.float32
    )
    residual = prediction - received_targets.reshape(-1, width).astype(jnp.float32)
    upstream = jnp.dot(
        residual.astype(jnp.bfloat16), expert_weight, preferred_element_type=jnp.float32
    )
    grad = norm_backward(upstream, normed, inputs).astype(jnp.bfloat16)
    return grad.reshape(groups, items, 2 * pred_size)


def general_shards(
    tokens, target_kv, context_kv, query_weight, pred_hidden, pred_weight, target_mask, owners
):
    new_kv = (
        keep_rate * target_kv.astype(jnp.float32)
        + (1.0 - keep_rate) * context_kv.astype(jnp.float32)
    ).astype(jnp.bfloat16)
    width = HEADS * HEAD
    scale = 1.0 / math.sqrt(HEAD)
    rows = tokens.shape[1]
    normed = layer_norm(tokens[0].astype(jnp.float32)).astype(jnp.bfloat16)
    queries = jnp.einsum(
        "td,ad->ta", normed, query_weight, preferred_element_type=jnp.float32
    ).astype(jnp.bfloat16)
    query_heads = queries.reshape(rows, HEADS, HEAD)
    own_kv = jnp.dot(
        normed,
        lax.all_gather(new_kv, "seq", axis=0, tiled=True),
        preferred_element_type=jnp.float32,
    ).astype(jnp.bfloat16)
    key_values = lax.all_gather(own_kv, "seq", axis=0, tiled=True)
    count = key_values.shape[0]
    keys = key_values[:, :width].reshape(count, HEADS, HEAD)
    values = key_values[:, width:].reshape(count, HEADS, HEAD)
    scores = (
        jnp.einsum("qhd,khd->hqk", query_heads, keys, preferred_element_type=jnp.float32) * scale
    )
    expo = jnp.exp(scores)
    added = jnp.einsum(
        "hqk,khd->qhd", expo.astype(jnp.bfloat16), values, preferred_element_type=jnp.float32
    )
    numerator = added.reshape(rows, width)
    denominator = jnp.sum(expo, axis=-1)
    attended = (numerator.reshape(rows, HEADS, HEAD) / denominator.T[:, :, None]).reshape(
        rows, width
    )
    targets = layer_norm(attended).astype(jnp.bfloat16)
    blocks = target_mask.shape[1]
    groups = lax.axis_size("grp")
    capacity = max(2, (blocks + groups - 1) // groups)
    pred_size = pred_hidden.shape[2]
    owner_ids = owners[0, :, 0]
    live = target_mask[0]
    chosen = (
        (owner_ids[:, None] == jnp.arange(groups, dtype=jnp.int32)[None, :]) & (live[:, None] == 1)
    ).astype(jnp.int32)
    earlier = jnp.cumsum(chosen, axis=0) - chosen
    position = jnp.sum(earlier * chosen, axis=1)
    slot_index = owner_ids * capacity + position
    dispatch = (
        (jnp.arange(groups * capacity, dtype=jnp.int32)[:, None] == slot_index[None, :])
        & (live[None, :] == 1)
    ).astype(jnp.bfloat16)
    send_targets = (
        jnp.dot(dispatch, targets.reshape(blocks, 2 * width), preferred_element_type=jnp.float32)
        .astype(jnp.bfloat16)
        .reshape(groups, capacity, 2 * width)
    )
    send_hidden = (
        jnp.dot(
            dispatch,
            pred_hidden[0].reshape(blocks, 2 * pred_size),
            preferred_element_type=jnp.float32,
        )
        .astype(jnp.bfloat16)
        .reshape(groups, capacity, 2 * pred_size)
    )
    expert_weight = pred_weight[0]
    owner_grads = owner_compute(
        (
            lax.all_to_all(send_targets, "grp", split_axis=0, concat_axis=0, tiled=True),
            lax.all_to_all(send_hidden, "grp", split_axis=0, concat_axis=0, tiled=True),
        ),
        expert_weight,
    )
    back_grads = lax.all_to_all(owner_grads, "grp", split_axis=0, concat_axis=0, tiled=True)
    pair_grads = jnp.dot(
        dispatch.T,
        back_grads.reshape(groups * capacity, 2 * pred_size),
        preferred_element_type=jnp.float32,
    )
    pred_grad = pair_grads.astype(jnp.bfloat16).reshape(rows, pred_size)
    return (new_kv, targets[None], pred_grad[None])


LANES = 128
PAIR_BUDGET = 16 << 20
VM = pl.BlockSpec(memory_space=pltpu.VMEM)
HBM = pl.BlockSpec(memory_space=pltpu.HBM)


def local_call(body, outs, operands, specs=None, out_specs=None, cost=None, scratch=(), limit=4):
    return pl.pallas_call(
        body,
        out_shape=outs,
        in_specs=specs or [VM] * len(operands),
        out_specs=out_specs or jax.tree.map(lambda _: VM, outs),
        scratch_shapes=list(scratch),
        cost_estimate=cost,
        compiler_params=pltpu.CompilerParams(vmem_limit_bytes=limit << 20),
    )(*operands)


def shape_of(dims, kind=jnp.bfloat16):
    return jax.ShapeDtypeStruct(dims, kind)


def matmul_cost(rows, depth, columns, extra=0):
    return pl.CostEstimate(
        flops=2 * rows * depth * columns, bytes_accessed=2 * depth * columns, transcendentals=extra
    )


def chip_and_core():
    me = lax.axis_index("seq")
    return me // 2, lax.rem(me, 2)


def chip_tiles(tiles, is_first, with_values):
    lane = lax.broadcasted_iota(jnp.int32, tiles[0].shape, 1) < HEAD
    mixed = jnp.where(lane, tiles[5], tiles[2])
    first = [tiles[0], tiles[1], tiles[2]]
    second = [tiles[3], tiles[4], mixed]
    if with_values:
        first = first + tiles[5:8]
        second = second + tiles[8:11]
    own = [jnp.where(is_first, a, b) for a, b in zip(first, second)]
    other = [jnp.where(is_first, b, a) for a, b in zip(first, second)]
    return own, other


def norm_body(tokens, normed, keep, send):
    half = tokens.shape[1] // 2
    chip, _ = chip_and_core()
    values = layer_norm(tokens[...].astype(jnp.float32)).astype(jnp.bfloat16)
    normed[...] = values
    low, high = values[:, :half], values[:, half:]
    keep[...] = jnp.where(chip == 0, low, high)
    send[...] = jnp.where(chip == 0, high, low)


def split_product(rows, weight, own, other):
    chip, _ = chip_and_core()
    sums = jnp.dot(rows[...], weight[...], preferred_element_type=jnp.float32)
    tiles = [sums[:, t * LANES : (t + 1) * LANES] for t in range(sums.shape[1] // LANES)]
    mine, theirs = chip_tiles(tiles, chip == 0, True)
    for t in range(6):
        own[:, t * LANES : (t + 1) * LANES] = mine[t]
        other[:, t * LANES : (t + 1) * LANES] = theirs[t].astype(jnp.bfloat16)


def first_partial_body(
    own_weight, other_weight, rows, normed, query_weight, joined, own, q_own, send, stored, sem
):
    chip, core = chip_and_core()
    depth = own_weight.shape[0]
    store = pltpu.make_async_copy(own_weight, stored, sem)
    store.start()
    joined[pl.ds(pl.multiple_of(core * depth, 16), depth), :] = own_weight[...]
    joined[pl.ds(pl.multiple_of((1 - core) * depth, 16), depth), :] = other_weight[...]
    split_product(rows, joined, own, send)
    queries = lax.dot_general(
        normed[...], query_weight[...], (((1,), (1,)), ((), ())), preferred_element_type=jnp.float32
    ).astype(jnp.bfloat16).astype(jnp.float32) * (1.0 / math.sqrt(HEAD))
    full = queries.shape[1] // LANES
    tiles = [queries[:, t * LANES : (t + 1) * LANES] for t in range(full)]
    rest = queries[:, full * LANES :]
    tiles.append(jnp.concatenate([rest, jnp.zeros_like(rest)], axis=1))
    mine, theirs = chip_tiles(tiles, chip == 0, False)
    for t in range(3):
        q_own[:, t * LANES : (t + 1) * LANES] = mine[t].astype(jnp.bfloat16)
        send[:, (6 + t) * LANES : (7 + t) * LANES] = theirs[t].astype(jnp.bfloat16)
    store.wait()


def partial_body(rows, weight, own, other):
    split_product(rows, weight, own, other)


def add_keys(queries, kv_refs, slot):
    upper_lane = lax.broadcasted_iota(jnp.int32, (1, LANES), 1) >= HEAD
    tile, upper = slot // 2, slot % 2
    lane = upper_lane if upper else jnp.logical_not(upper_lane)
    q = queries[:, tile * LANES : (tile + 1) * LANES]
    q = jnp.where(lane, q, jnp.zeros_like(q))
    v_tile, v_upper = (slot + 1) % 6 // 2, (slot + 1) % 2
    v_lane = upper_lane if v_upper else jnp.logical_not(upper_lane)
    total = None
    for kv in kv_refs:
        keys = kv[:, tile * LANES : (tile + 1) * LANES]
        scores = lax.dot_general(
            q, keys, (((1,), (1,)), ((), ())), preferred_element_type=jnp.float32
        )
        weights = jnp.exp(scores).astype(jnp.bfloat16)
        start = (3 + v_tile) * LANES
        values = kv[:, start : start + LANES]
        values = jnp.where(v_lane, values, jnp.ones_like(values))
        part = jnp.dot(weights, values, preferred_element_type=jnp.float32)
        total = part if total is None else total + part
    return total


def attend_first_body(q_own, received, kv_a, kv_b, own_sums, other_sums):
    q_other = received[:, 6 * LANES :]
    for slot in range(6):
        own_sums[slot] = add_keys(q_own, (kv_a, kv_b), slot)
        other_sums[slot] = add_keys(q_other, (kv_a, kv_b), slot)


def attend_last_body(q_own, received, kv_a, kv_b, own_sums, other_sums, mine, theirs):
    upper_lane = lax.broadcasted_iota(jnp.int32, (1, LANES), 1) >= HEAD
    q_other = received[:, 6 * LANES :]
    for queries, sums, out in ((q_other, other_sums, theirs), (q_own, own_sums, mine)):
        found = [None] * 6
        for slot in range(6):
            total = sums[slot] + add_keys(queries, (kv_a, kv_b), slot)
            found[(slot + 1) % 6] = total / pltpu.roll(total, HEAD, 1)
        for t in range(3):
            joined = jnp.where(upper_lane, found[2 * t + 1], found[2 * t])
            out[:, t * LANES : (t + 1) * LANES] = joined.astype(out.dtype)


def token_values(pairs, rows):
    shape = (rows, pairs.shape[1])
    token = lax.broadcasted_iota(jnp.int32, shape, 0) // 2
    pair = lax.broadcasted_iota(jnp.int32, shape, 1)
    values = jnp.where(token == pair, pairs[...], 0)
    return jnp.sum(values, axis=1, keepdims=True)


def owner_at(moved, groups):
    me = lax.axis_index("grp")
    place = jnp.where(lax.rem(me, 2) == 0, me // 2, groups - 1 - me // 2)
    place = lax.rem(place + moved + groups, groups)
    return jnp.where(place < groups // 2, 2 * place, 2 * (groups - 1 - place) + 1)


def slot_owners(groups):
    _, core = chip_and_core()
    sign = 2 * core - 1
    owners = [owner_at(0, groups)]
    for step in range(1, groups // 2):
        owners += [owner_at(sign * step, groups), owner_at(-sign * step, groups)]
    return owners + [owner_at(groups // 2, groups)]


def join_halves(mine, theirs, joined):
    _, core = chip_and_core()
    rows = mine.shape[0]
    joined[pl.ds(pl.multiple_of(core * rows, 16), rows), :] = mine[...]
    joined[pl.ds(pl.multiple_of((1 - core) * rows, 16), rows), :] = theirs[...]


def add_predictions(owners, hidden, weights, ids_of):
    normed = layer_norm(hidden[...].astype(jnp.float32)).astype(jnp.bfloat16)
    ids = token_values(owners, hidden.shape[0])
    total = None
    for weight, owner in zip(weights, ids_of):
        picked = jnp.where(ids == owner, normed, jnp.zeros_like(normed))
        part = lax.dot_general(
            picked, weight[...], (((1,), (1,)), ((), ())), preferred_element_type=jnp.float32
        )
        total = part if total is None else total + part
    return total


def predict_body(groups, owners, hidden, *refs):
    weights, prediction = refs[:-1], refs[-1]
    prediction[...] = add_predictions(owners, hidden, weights, slot_owners(groups))


def predict_last_body(groups, owners, hidden, earlier, mine, theirs, *refs):
    weights, (prediction, joined) = refs[:-2], refs[-2:]
    join_halves(mine, theirs, joined)
    places = slot_owners(groups)[groups - 1 - len(weights) :]
    prediction[...] = earlier[...] + add_predictions(
        owners, hidden, (*weights, joined), places
    )


def finish_body(owners, mask, attended, returned, prediction, hidden, *refs):
    weights, (targets, grad) = refs[:-2], refs[-2:]
    chip, _ = chip_and_core()
    width, rows = targets.shape
    mine, theirs = attended[...], returned[...].astype(jnp.float32)
    joined = jnp.concatenate(
        [jnp.where(chip == 0, mine, theirs), jnp.where(chip == 0, theirs, mine)], axis=1
    )
    lane = lax.broadcasted_iota(jnp.int32, joined.shape, 1) >= HEAD
    joined = jnp.where(lane, joined, 0.0)
    mean = jnp.sum(joined, axis=1, keepdims=True) * (1.0 / width)
    center = jnp.where(lane, joined - mean, 0.0)
    variance = jnp.sum(center * center, axis=1, keepdims=True) * (1.0 / width)
    found = (center * lax.rsqrt(variance + epsilon))[:, HEAD:].astype(jnp.bfloat16)
    targets[...] = found.T
    residual = (prediction[...] - found.astype(jnp.float32)).astype(jnp.bfloat16)
    ids = token_values(owners, rows)
    upstream = jnp.zeros(hidden.shape, jnp.float32)
    for weight, owner in zip(weights, slot_owners(len(weights))):
        picked = jnp.where(ids == owner, residual, jnp.zeros_like(residual))
        upstream = upstream + jnp.dot(picked, weight[...], preferred_element_type=jnp.float32)
    inputs = hidden[...].astype(jnp.float32)
    back = norm_backward(upstream, layer_norm(inputs), inputs)
    grad[...] = jnp.where(token_values(mask, rows) == 1, back, 0.0).astype(grad.dtype)


def ring_pairs(members, groups):
    order = list(range(0, groups, 2)) + list(range(groups - 1, 0, -2))
    pairs = []
    for member in range(members):
        for i in range(groups):
            a, b = order[i], order[(i + 1) % groups]
            a, b = (a, b) if member % 2 == 0 else (b, a)
            pairs.append((member * groups + a, member * groups + b))
    return pairs


def paired_shards(
    tokens, target_kv, context_kv, query_weight, pred_hidden, pred_weight, target_mask, owners
):
    members = lax.axis_size("seq")
    groups = lax.axis_size("grp")
    across = [(i, (i + members // 2) % members) for i in range(members)]
    beside = [(i, i ^ 1) for i in range(members)]
    ring = ring_pairs(members, groups)
    core = lax.rem(lax.axis_index("seq"), 2)
    rows, width = tokens.shape[1], query_weight.shape[0]
    features = tokens.shape[2]
    half = features // 2
    packed = 3 * LANES
    out_rows, pred_size = pred_weight.shape[1:]
    owner_row, mask_row = owners.reshape(1, -1), target_mask.reshape(1, -1)
    sums_shape = shape_of((rows, 2 * packed), jnp.float32)

    normed, keep, send = local_call(
        norm_body,
        [shape_of((rows, features)), shape_of((rows, half)), shape_of((rows, half))],
        (tokens[0],),
    )
    kept_other = lax.ppermute(send, "seq", across)
    new_kv = (
        keep_rate * target_kv.astype(jnp.float32)
        + (1.0 - keep_rate) * context_kv.astype(jnp.float32)
    ).astype(jnp.bfloat16)
    other_kv = lax.ppermute(new_kv, "seq", beside)
    joined, own_sum, q_own, own_send, stored_kv = local_call(
        first_partial_body,
        [
            shape_of((half, 2 * width)),
            sums_shape,
            shape_of((rows, packed)),
            shape_of((rows, 3 * packed)),
            shape_of(target_kv.shape),
        ],
        (new_kv, other_kv, keep, normed, query_weight),
        out_specs=[VM] * 4 + [HBM],
        scratch=[pltpu.SemaphoreType.DMA],
        cost=matmul_cost(rows, half, 4 * width),
    )
    received = lax.ppermute(own_send, "seq", across)
    other_sum, other_send = local_call(
        partial_body,
        [sums_shape, shape_of((rows, 2 * packed))],
        (kept_other, joined),
        cost=matmul_cost(rows, half, 2 * width),
    )
    from_other = lax.ppermute(other_send, "seq", across)
    kv_a = (other_sum + received[:, : 2 * packed].astype(jnp.float32)).astype(jnp.bfloat16)
    kv_a_beside = lax.ppermute(kv_a, "seq", beside)
    all_sums = shape_of((6, rows, LANES), jnp.float32)
    own_sums, other_sums = local_call(
        attend_first_body,
        [all_sums, all_sums],
        (q_own, received, kv_a, kv_a_beside),
        cost=matmul_cost(2 * rows, 12 * LANES, 2 * rows, 12 * rows * 2 * rows),
    )
    kv_b = (own_sum + from_other.astype(jnp.float32)).astype(jnp.bfloat16)
    kv_b_beside = lax.ppermute(kv_b, "seq", beside)
    attended, send_back = local_call(
        attend_last_body,
        [shape_of((rows, packed), jnp.float32), shape_of((rows, packed))],
        (q_own, received, kv_b, kv_b_beside, own_sums, other_sums),
        cost=matmul_cost(2 * rows, 12 * LANES, 2 * rows, 12 * rows * 2 * rows),
    )
    returned = lax.ppermute(send_back, "seq", across)

    weights = [pred_weight[0]]
    held = pred_weight[0]
    for _ in range(1, groups // 2):
        held = lax.ppermute(held, ("seq", "grp"), ring)
        weights += [held, lax.ppermute(held, "seq", beside)]
    half_rows = out_rows // 2
    held = lax.dynamic_slice(held, (core * half_rows, 0), (half_rows, pred_size))
    mine = lax.ppermute(held, ("seq", "grp"), ring)
    theirs = lax.ppermute(mine, "seq", beside)
    early = max(1, len(weights) - 2)
    prediction = local_call(
        functools.partial(predict_body, groups),
        shape_of((rows, width), jnp.float32),
        (owner_row, pred_hidden[0], *weights[:early]),
        cost=matmul_cost(rows, early * pred_size, width),
    )
    prediction, opposite = local_call(
        functools.partial(predict_last_body, groups),
        [shape_of((rows, width), jnp.float32), shape_of((out_rows, pred_size))],
        (owner_row, pred_hidden[0], prediction, mine, theirs, *weights[early:]),
        cost=matmul_cost(rows, 3 * pred_size, width),
    )
    targets, grad = local_call(
        finish_body,
        [shape_of((width, rows)), shape_of((rows, pred_size))],
        (
            owner_row, mask_row, attended, returned, prediction, pred_hidden[0],
            *weights, opposite,
        ),
        out_specs=[pl.BlockSpec(), pl.BlockSpec()],
        cost=matmul_cost(rows, groups * pred_size, width),
    )
    return (stored_kv, targets.T[None], grad[None])


def shards(*arguments):
    pred_weight = arguments[5]
    gathered = lax.axis_size("grp") * pred_weight.size * pred_weight.dtype.itemsize
    two_chips = lax.axis_size("seq") == 4
    if two_chips and lax.axis_size("grp") % 2 == 0 and gathered <= PAIR_BUDGET:
        return paired_shards(*arguments)
    return general_shards(*arguments)


def solution(mesh):
    placed = (
        P("grp", "seq", None),
        P("seq", None),
        P("seq", None),
        P(),
        P("grp", "seq", None),
        P("grp", None, None),
        P("grp", "seq"),
        P("grp", "seq", None),
    )
    return jax.shard_map(
        shards,
        mesh=mesh,
        in_specs=placed,
        out_specs=(P("seq", None), P("grp", "seq", None), P("grp", "seq", None)),
        check_vma=False,
    )
```

```python
import functools
import math

import jax
import jax.numpy as jnp
from jax import lax
from jax.experimental import pallas as pl
from jax.experimental.pallas import tpu as pltpu
from jax.sharding import PartitionSpec as P


HEAD = 64
HEADS = 11


keep_rate = 0.9
epsilon = 1e-05


def layer_norm(values):
    center = values - jnp.mean(values, axis=-1, keepdims=True)
    variance = jnp.mean(center * center, axis=-1, keepdims=True)
    return center * lax.rsqrt(variance + epsilon)


def norm_backward(upstream, normed, inputs):
    center = inputs - jnp.mean(inputs, axis=-1, keepdims=True)
    variance = jnp.mean(center * center, axis=-1, keepdims=True)
    inverse = lax.rsqrt(variance + epsilon)
    upstream_mean = jnp.mean(upstream, axis=-1, keepdims=True)
    cross_mean = jnp.mean(upstream * normed, axis=-1, keepdims=True)
    return inverse * (upstream - upstream_mean - normed * cross_mean)


def owner_compute(received, expert_weight):
    received_targets, received_hidden = received
    groups = received_targets.shape[0]
    items = received_targets.shape[1]
    pred_size = expert_weight.shape[1]
    width = expert_weight.shape[0]
    inputs = received_hidden.reshape(-1, pred_size).astype(jnp.float32)
    normed = layer_norm(inputs)
    prediction = jnp.einsum(
        "tp,ap->ta", normed.astype(jnp.bfloat16), expert_weight, preferred_element_type=jnp.float32
    )
    residual = prediction - received_targets.reshape(-1, width).astype(jnp.float32)
    upstream = jnp.dot(
        residual.astype(jnp.bfloat16), expert_weight, preferred_element_type=jnp.float32
    )
    grad = norm_backward(upstream, normed, inputs).astype(jnp.bfloat16)
    return grad.reshape(groups, items, 2 * pred_size)


def general_shards(
    tokens, target_kv, context_kv, query_weight, pred_hidden, pred_weight, target_mask, owners
):
    new_kv = (
        keep_rate * target_kv.astype(jnp.float32)
        + (1.0 - keep_rate) * context_kv.astype(jnp.float32)
    ).astype(jnp.bfloat16)
    width = HEADS * HEAD
    scale = 1.0 / math.sqrt(HEAD)
    rows = tokens.shape[1]
    normed = layer_norm(tokens[0].astype(jnp.float32)).astype(jnp.bfloat16)
    queries = jnp.einsum(
        "td,ad->ta", normed, query_weight, preferred_element_type=jnp.float32
    ).astype(jnp.bfloat16)
    query_heads = queries.reshape(rows, HEADS, HEAD)
    own_kv = jnp.dot(
        normed,
        lax.all_gather(new_kv, "seq", axis=0, tiled=True),
        preferred_element_type=jnp.float32,
    ).astype(jnp.bfloat16)
    key_values = lax.all_gather(own_kv, "seq", axis=0, tiled=True)
    count = key_values.shape[0]
    keys = key_values[:, :width].reshape(count, HEADS, HEAD)
    values = key_values[:, width:].reshape(count, HEADS, HEAD)
    scores = (
        jnp.einsum("qhd,khd->hqk", query_heads, keys, preferred_element_type=jnp.float32) * scale
    )
    expo = jnp.exp(scores)
    added = jnp.einsum(
        "hqk,khd->qhd", expo.astype(jnp.bfloat16), values, preferred_element_type=jnp.float32
    )
    numerator = added.reshape(rows, width)
    denominator = jnp.sum(expo, axis=-1)
    attended = (numerator.reshape(rows, HEADS, HEAD) / denominator.T[:, :, None]).reshape(
        rows, width
    )
    targets = layer_norm(attended).astype(jnp.bfloat16)
    blocks = target_mask.shape[1]
    groups = lax.axis_size("grp")
    capacity = max(2, (blocks + groups - 1) // groups)
    pred_size = pred_hidden.shape[2]
    owner_ids = owners[0, :, 0]
    live = target_mask[0]
    chosen = (
        (owner_ids[:, None] == jnp.arange(groups, dtype=jnp.int32)[None, :]) & (live[:, None] == 1)
    ).astype(jnp.int32)
    earlier = jnp.cumsum(chosen, axis=0) - chosen
    position = jnp.sum(earlier * chosen, axis=1)
    slot_index = owner_ids * capacity + position
    dispatch = (
        (jnp.arange(groups * capacity, dtype=jnp.int32)[:, None] == slot_index[None, :])
        & (live[None, :] == 1)
    ).astype(jnp.bfloat16)
    send_targets = (
        jnp.dot(dispatch, targets.reshape(blocks, 2 * width), preferred_element_type=jnp.float32)
        .astype(jnp.bfloat16)
        .reshape(groups, capacity, 2 * width)
    )
    send_hidden = (
        jnp.dot(
            dispatch,
            pred_hidden[0].reshape(blocks, 2 * pred_size),
            preferred_element_type=jnp.float32,
        )
        .astype(jnp.bfloat16)
        .reshape(groups, capacity, 2 * pred_size)
    )
    expert_weight = pred_weight[0]
    owner_grads = owner_compute(
        (
            lax.all_to_all(send_targets, "grp", split_axis=0, concat_axis=0, tiled=True),
            lax.all_to_all(send_hidden, "grp", split_axis=0, concat_axis=0, tiled=True),
        ),
        expert_weight,
    )
    back_grads = lax.all_to_all(owner_grads, "grp", split_axis=0, concat_axis=0, tiled=True)
    pair_grads = jnp.dot(
        dispatch.T,
        back_grads.reshape(groups * capacity, 2 * pred_size),
        preferred_element_type=jnp.float32,
    )
    pred_grad = pair_grads.astype(jnp.bfloat16).reshape(rows, pred_size)
    return (new_kv, targets[None], pred_grad[None])


LANES = 128
PAIR_BUDGET = 16 << 20
VM = pl.BlockSpec(memory_space=pltpu.VMEM)
HBM = pl.BlockSpec(memory_space=pltpu.HBM)


def local_call(body, outs, operands, specs=None, out_specs=None, cost=None, scratch=(), limit=4):
    return pl.pallas_call(
        body,
        out_shape=outs,
        in_specs=specs or [VM] * len(operands),
        out_specs=out_specs or jax.tree.map(lambda _: VM, outs),
        scratch_shapes=list(scratch),
        cost_estimate=cost,
        compiler_params=pltpu.CompilerParams(vmem_limit_bytes=limit << 20),
    )(*operands)


def shape_of(dims, kind=jnp.bfloat16):
    return jax.ShapeDtypeStruct(dims, kind)


def matmul_cost(rows, depth, columns, extra=0):
    return pl.CostEstimate(
        flops=2 * rows * depth * columns, bytes_accessed=2 * depth * columns, transcendentals=extra
    )


def chip_and_core():
    me = lax.axis_index("seq")
    return me // 2, lax.rem(me, 2)


def chip_tiles(tiles, is_first, with_values):
    lane = lax.broadcasted_iota(jnp.int32, tiles[0].shape, 1) < HEAD
    mixed = jnp.where(lane, tiles[5], tiles[2])
    first = [tiles[0], tiles[1], tiles[2]]
    second = [tiles[3], tiles[4], mixed]
    if with_values:
        first = first + tiles[5:8]
        second = second + tiles[8:11]
    own = [jnp.where(is_first, a, b) for a, b in zip(first, second)]
    other = [jnp.where(is_first, b, a) for a, b in zip(first, second)]
    return own, other


def norm_body(tokens, normed, keep, send):
    half = tokens.shape[1] // 2
    chip, _ = chip_and_core()
    values = layer_norm(tokens[...].astype(jnp.float32)).astype(jnp.bfloat16)
    normed[...] = values
    low, high = values[:, :half], values[:, half:]
    keep[...] = jnp.where(chip == 0, low, high)
    send[...] = jnp.where(chip == 0, high, low)


def split_product(rows, weight, own, other):
    chip, _ = chip_and_core()
    sums = jnp.dot(rows[...], weight[...], preferred_element_type=jnp.float32)
    tiles = [sums[:, t * LANES : (t + 1) * LANES] for t in range(sums.shape[1] // LANES)]
    mine, theirs = chip_tiles(tiles, chip == 0, True)
    for t in range(6):
        own[:, t * LANES : (t + 1) * LANES] = mine[t]
        other[:, t * LANES : (t + 1) * LANES] = theirs[t].astype(jnp.bfloat16)


def blend(target, context):
    return (
        keep_rate * target[...].astype(jnp.float32)
        + (1.0 - keep_rate) * context[...].astype(jnp.float32)
    ).astype(jnp.bfloat16)


def first_partial_body(
    target, context, other_target, other_context, rows, normed, query_weight,
    joined, own, q_own, send, stored, sem,
):
    chip, core = chip_and_core()
    depth = target.shape[0]
    own_rows = pl.ds(pl.multiple_of(core * depth, 16), depth)
    joined[own_rows, :] = blend(target, context)
    store = pltpu.make_async_copy(joined.at[own_rows], stored, sem)
    store.start()
    joined[pl.ds(pl.multiple_of((1 - core) * depth, 16), depth), :] = blend(
        other_target, other_context
    )
    split_product(rows, joined, own, send)
    queries = lax.dot_general(
        normed[...], query_weight[...], (((1,), (1,)), ((), ())), preferred_element_type=jnp.float32
    ).astype(jnp.bfloat16).astype(jnp.float32) * (1.0 / math.sqrt(HEAD))
    full = queries.shape[1] // LANES
    tiles = [queries[:, t * LANES : (t + 1) * LANES] for t in range(full)]
    rest = queries[:, full * LANES :]
    tiles.append(jnp.concatenate([rest, jnp.zeros_like(rest)], axis=1))
    mine, theirs = chip_tiles(tiles, chip == 0, False)
    for t in range(3):
        q_own[:, t * LANES : (t + 1) * LANES] = mine[t].astype(jnp.bfloat16)
        send[:, (6 + t) * LANES : (7 + t) * LANES] = theirs[t].astype(jnp.bfloat16)
    store.wait()


def partial_body(rows, weight, own, other):
    split_product(rows, weight, own, other)


def add_keys(queries, kv_refs, slot):
    upper_lane = lax.broadcasted_iota(jnp.int32, (1, LANES), 1) >= HEAD
    tile, upper = slot // 2, slot % 2
    lane = upper_lane if upper else jnp.logical_not(upper_lane)
    q = queries[:, tile * LANES : (tile + 1) * LANES]
    q = jnp.where(lane, q, jnp.zeros_like(q))
    v_tile, v_upper = (slot + 1) % 6 // 2, (slot + 1) % 2
    v_lane = upper_lane if v_upper else jnp.logical_not(upper_lane)
    total = None
    for kv in kv_refs:
        keys = kv[:, tile * LANES : (tile + 1) * LANES]
        scores = lax.dot_general(
            q, keys, (((1,), (1,)), ((), ())), preferred_element_type=jnp.float32
        )
        weights = jnp.exp(scores).astype(jnp.bfloat16)
        start = (3 + v_tile) * LANES
        values = kv[:, start : start + LANES]
        values = jnp.where(v_lane, values, jnp.ones_like(values))
        part = jnp.dot(weights, values, preferred_element_type=jnp.float32)
        total = part if total is None else total + part
    return total


def attend_body(queries, kv_a, kv_b, mine, theirs):
    upper_lane = lax.broadcasted_iota(jnp.int32, (1, LANES), 1) >= HEAD
    rows = mine.shape[0]
    found = [None] * 6
    for slot in range(6):
        total = add_keys(queries, (kv_a, kv_b), slot)
        found[(slot + 1) % 6] = total / pltpu.roll(total, HEAD, 1)
    for t in range(3):
        joined = jnp.where(upper_lane, found[2 * t + 1], found[2 * t])
        mine[:, t * LANES : (t + 1) * LANES] = joined[:rows]
        theirs[:, t * LANES : (t + 1) * LANES] = joined[rows:].astype(theirs.dtype)


def token_values(pairs, rows):
    shape = (rows, pairs.shape[1])
    token = lax.broadcasted_iota(jnp.int32, shape, 0) // 2
    pair = lax.broadcasted_iota(jnp.int32, shape, 1)
    values = jnp.where(token == pair, pairs[...], 0)
    return jnp.sum(values, axis=1, keepdims=True)


def owner_at(moved, groups):
    me = lax.axis_index("grp")
    place = jnp.where(lax.rem(me, 2) == 0, me // 2, groups - 1 - me // 2)
    place = lax.rem(place + moved + groups, groups)
    return jnp.where(place < groups // 2, 2 * place, 2 * (groups - 1 - place) + 1)


def slot_owners(groups):
    _, core = chip_and_core()
    sign = 2 * core - 1
    owners = [owner_at(0, groups)]
    for step in range(1, groups // 2):
        owners += [owner_at(sign * step, groups), owner_at(-sign * step, groups)]
    return owners + [owner_at(groups // 2, groups)]


def join_halves(mine, theirs, joined):
    _, core = chip_and_core()
    rows = mine.shape[0]
    joined[pl.ds(pl.multiple_of(core * rows, 16), rows), :] = mine[...]
    joined[pl.ds(pl.multiple_of((1 - core) * rows, 16), rows), :] = theirs[...]


def add_predictions(owners, hidden, weights, ids_of):
    normed = layer_norm(hidden[...].astype(jnp.float32)).astype(jnp.bfloat16)
    ids = token_values(owners, hidden.shape[0])
    total = None
    for weight, owner in zip(weights, ids_of):
        picked = jnp.where(ids == owner, normed, jnp.zeros_like(normed))
        part = lax.dot_general(
            picked, weight[...], (((1,), (1,)), ((), ())), preferred_element_type=jnp.float32
        )
        total = part if total is None else total + part
    return total


def predict_body(groups, owners, hidden, *refs):
    weights, prediction = refs[:-1], refs[-1]
    prediction[...] = add_predictions(owners, hidden, weights, slot_owners(groups))


def predict_rest_body(groups, owners, hidden, earlier, mine, theirs, *refs):
    weights, (prediction, joined) = refs[:-2], refs[-2:]
    join_halves(mine, theirs, joined)
    places = slot_owners(groups)[groups - 1 - len(weights) :]
    prediction[...] = earlier[...] + add_predictions(owners, hidden, (*weights, joined), places)


def cut_body(whole, first, second):
    _, core = chip_and_core()
    rows = first.shape[0]
    first[...] = whole[pl.ds(pl.multiple_of(core * rows, 16), rows), :]
    second[...] = whole[pl.ds(pl.multiple_of((1 - core) * rows, 16), rows), :]


def join_body(first, second, joined):
    join_halves(first, second, joined)


def add_upstream(residual, ids, weights, ids_of):
    total = None
    for weight, owner in zip(weights, ids_of):
        picked = jnp.where(ids == owner, residual, jnp.zeros_like(residual))
        part = jnp.dot(picked, weight[...], preferred_element_type=jnp.float32)
        total = part if total is None else total + part
    return total


def finish_body(groups, owners, mask, attended, returned, prediction, hidden, *refs):
    weights, (targets, grad) = refs[:-2], refs[-2:]
    chip, _ = chip_and_core()
    width, rows = targets.shape
    mine, theirs = attended[...], returned[...].astype(jnp.float32)
    joined = jnp.concatenate(
        [jnp.where(chip == 0, mine, theirs), jnp.where(chip == 0, theirs, mine)], axis=1
    )
    lane = lax.broadcasted_iota(jnp.int32, joined.shape, 1) >= HEAD
    joined = jnp.where(lane, joined, 0.0)
    mean = jnp.sum(joined, axis=1, keepdims=True) * (1.0 / width)
    center = jnp.where(lane, joined - mean, 0.0)
    variance = jnp.sum(center * center, axis=1, keepdims=True) * (1.0 / width)
    found = (center * lax.rsqrt(variance + epsilon))[:, HEAD:].astype(jnp.bfloat16)
    targets[...] = found.T
    residual = (prediction[...] - found.astype(jnp.float32)).astype(jnp.bfloat16)
    ids = token_values(owners, rows)
    upstream = add_upstream(residual, ids, weights, slot_owners(groups))
    inputs = hidden[...].astype(jnp.float32)
    back = norm_backward(upstream, layer_norm(inputs), inputs)
    grad[...] = jnp.where(token_values(mask, rows) == 1, back, 0.0).astype(grad.dtype)


def ring_pairs(members, groups):
    order = list(range(0, groups, 2)) + list(range(groups - 1, 0, -2))
    pairs = []
    for member in range(members):
        for i in range(groups):
            a, b = order[i], order[(i + 1) % groups]
            a, b = (a, b) if member % 2 == 0 else (b, a)
            pairs.append((member * groups + a, member * groups + b))
    return pairs


def paired_shards(
    tokens, target_kv, context_kv, query_weight, pred_hidden, pred_weight, target_mask, owners
):
    members = lax.axis_size("seq")
    groups = lax.axis_size("grp")
    across = [(i, (i + members // 2) % members) for i in range(members)]
    beside = [(i, i ^ 1) for i in range(members)]
    ring = ring_pairs(members, groups)
    rows, width = tokens.shape[1], query_weight.shape[0]
    features = tokens.shape[2]
    half = features // 2
    packed = 3 * LANES
    out_rows, pred_size = pred_weight.shape[1:]
    owner_row, mask_row = owners.reshape(1, -1), target_mask.reshape(1, -1)
    sums_shape = shape_of((rows, 2 * packed), jnp.float32)

    other_target = lax.ppermute(target_kv, "seq", beside)
    other_context = lax.ppermute(context_kv, "seq", beside)
    normed, keep, send = local_call(
        norm_body,
        [shape_of((rows, features)), shape_of((rows, half)), shape_of((rows, half))],
        (tokens[0],),
        cost=pl.CostEstimate(flops=1 << 33, bytes_accessed=1 << 20, transcendentals=0),
    )
    kept_other = lax.ppermute(send, "seq", across)
    joined, own_sum, q_own, own_send, stored_kv = local_call(
        first_partial_body,
        [
            shape_of((half, 2 * width)),
            sums_shape,
            shape_of((rows, packed)),
            shape_of((rows, 3 * packed)),
            shape_of(target_kv.shape),
        ],
        (target_kv, context_kv, other_target, other_context, keep, normed, query_weight),
        out_specs=[VM] * 4 + [HBM],
        scratch=[pltpu.SemaphoreType.DMA],
        cost=matmul_cost(rows, half, 4 * width),
    )
    received = lax.ppermute(own_send, "seq", across)
    other_sum, other_send = local_call(
        partial_body,
        [sums_shape, shape_of((rows, 2 * packed))],
        (kept_other, joined),
        cost=matmul_cost(rows, half, 2 * width),
    )
    from_other = lax.ppermute(other_send, "seq", across)
    kv = jnp.concatenate(
        [
            (other_sum + received[:, : 2 * packed].astype(jnp.float32)).astype(jnp.bfloat16),
            (own_sum + from_other.astype(jnp.float32)).astype(jnp.bfloat16),
        ],
        axis=0,
    )
    kv_beside = lax.ppermute(kv, "seq", beside)
    queries = jnp.concatenate([q_own, received[:, 2 * packed :]], axis=0)
    attended, send_back = local_call(
        attend_body,
        [shape_of((rows, packed), jnp.float32), shape_of((rows, packed))],
        (queries, kv, kv_beside),
        cost=matmul_cost(2 * rows, 12 * LANES, 4 * rows, 12 * rows * 4 * rows),
    )
    returned = lax.ppermute(send_back, "seq", across)

    half_rows = out_rows // 2
    half_shape, whole_shape = shape_of((half_rows, pred_size)), shape_of((out_rows, pred_size))
    halves = [half_shape, half_shape]
    weights = [pred_weight[0]]
    last_step = groups // 2
    for step in range(1, last_step):
        if step == 1:
            held = lax.ppermute(pred_weight[0], ("seq", "grp"), ring)
            first, second = local_call(cut_body, halves, (held,))
        else:
            first = lax.ppermute(first, ("seq", "grp"), ring)
            second = lax.ppermute(second, ("seq", "grp"), ring)
            held = local_call(join_body, whole_shape, (first, second))
        weights += [held, lax.ppermute(held, "seq", beside)]
    if last_step == 1:
        first, second = local_call(cut_body, halves, (pred_weight[0],))
    mine = lax.ppermute(first, ("seq", "grp"), ring)
    theirs = lax.ppermute(mine, "seq", beside)
    early = max(1, len(weights) - 2)
    prediction = local_call(
        functools.partial(predict_body, groups),
        shape_of((rows, width), jnp.float32),
        (owner_row, pred_hidden[0], *weights[:early]),
        cost=matmul_cost(rows, early * pred_size, width),
    )
    prediction, opposite = local_call(
        functools.partial(predict_rest_body, groups),
        [shape_of((rows, width), jnp.float32), whole_shape],
        (owner_row, pred_hidden[0], prediction, mine, theirs, *weights[early:]),
        cost=matmul_cost(rows, (groups - early) * pred_size, width),
    )
    weights.append(opposite)
    targets, grad = local_call(
        functools.partial(finish_body, groups),
        [shape_of((width, rows)), shape_of((rows, pred_size))],
        (owner_row, mask_row, attended, returned, prediction, pred_hidden[0], *weights),
        out_specs=[pl.BlockSpec(), pl.BlockSpec()],
        cost=matmul_cost(rows, groups * pred_size, width),
    )
    return (stored_kv, targets.T[None], grad[None])


def shards(*arguments):
    pred_weight = arguments[5]
    gathered = lax.axis_size("grp") * pred_weight.size * pred_weight.dtype.itemsize
    two_chips = lax.axis_size("seq") == 4
    if two_chips and lax.axis_size("grp") % 2 == 0 and gathered <= PAIR_BUDGET:
        return paired_shards(*arguments)
    return general_shards(*arguments)


def solution(mesh):
    placed = (
        P("grp", "seq", None),
        P("seq", None),
        P("seq", None),
        P(),
        P("grp", "seq", None),
        P("grp", None, None),
        P("grp", "seq"),
        P("grp", "seq", None),
    )
    return jax.shard_map(
        shards,
        mesh=mesh,
        in_specs=placed,
        out_specs=(P("seq", None), P("grp", "seq", None), P("grp", "seq", None)),
        check_vma=False,
    )
```

```python
import functools
import math

import jax
import jax.numpy as jnp
from jax import lax
from jax.experimental import pallas as pl
from jax.experimental.pallas import tpu as pltpu
from jax.sharding import PartitionSpec as P


HEAD = 64
HEADS = 11


keep_rate = 0.9
epsilon = 1e-05


def layer_norm(values):
    center = values - jnp.mean(values, axis=-1, keepdims=True)
    variance = jnp.mean(center * center, axis=-1, keepdims=True)
    return center * lax.rsqrt(variance + epsilon)


def norm_backward(upstream, normed, inputs):
    center = inputs - jnp.mean(inputs, axis=-1, keepdims=True)
    variance = jnp.mean(center * center, axis=-1, keepdims=True)
    inverse = lax.rsqrt(variance + epsilon)
    upstream_mean = jnp.mean(upstream, axis=-1, keepdims=True)
    cross_mean = jnp.mean(upstream * normed, axis=-1, keepdims=True)
    return inverse * (upstream - upstream_mean - normed * cross_mean)


def owner_compute(received, expert_weight):
    received_targets, received_hidden = received
    groups = received_targets.shape[0]
    items = received_targets.shape[1]
    pred_size = expert_weight.shape[1]
    width = expert_weight.shape[0]
    inputs = received_hidden.reshape(-1, pred_size).astype(jnp.float32)
    normed = layer_norm(inputs)
    prediction = jnp.einsum(
        "tp,ap->ta", normed.astype(jnp.bfloat16), expert_weight, preferred_element_type=jnp.float32
    )
    residual = prediction - received_targets.reshape(-1, width).astype(jnp.float32)
    upstream = jnp.dot(
        residual.astype(jnp.bfloat16), expert_weight, preferred_element_type=jnp.float32
    )
    grad = norm_backward(upstream, normed, inputs).astype(jnp.bfloat16)
    return grad.reshape(groups, items, 2 * pred_size)


def general_shards(
    tokens, target_kv, context_kv, query_weight, pred_hidden, pred_weight, target_mask, owners
):
    new_kv = (
        keep_rate * target_kv.astype(jnp.float32)
        + (1.0 - keep_rate) * context_kv.astype(jnp.float32)
    ).astype(jnp.bfloat16)
    width = HEADS * HEAD
    scale = 1.0 / math.sqrt(HEAD)
    rows = tokens.shape[1]
    normed = layer_norm(tokens[0].astype(jnp.float32)).astype(jnp.bfloat16)
    queries = jnp.einsum(
        "td,ad->ta", normed, query_weight, preferred_element_type=jnp.float32
    ).astype(jnp.bfloat16)
    query_heads = queries.reshape(rows, HEADS, HEAD)
    own_kv = jnp.dot(
        normed,
        lax.all_gather(new_kv, "seq", axis=0, tiled=True),
        preferred_element_type=jnp.float32,
    ).astype(jnp.bfloat16)
    key_values = lax.all_gather(own_kv, "seq", axis=0, tiled=True)
    count = key_values.shape[0]
    keys = key_values[:, :width].reshape(count, HEADS, HEAD)
    values = key_values[:, width:].reshape(count, HEADS, HEAD)
    scores = (
        jnp.einsum("qhd,khd->hqk", query_heads, keys, preferred_element_type=jnp.float32) * scale
    )
    expo = jnp.exp(scores)
    added = jnp.einsum(
        "hqk,khd->qhd", expo.astype(jnp.bfloat16), values, preferred_element_type=jnp.float32
    )
    numerator = added.reshape(rows, width)
    denominator = jnp.sum(expo, axis=-1)
    attended = (numerator.reshape(rows, HEADS, HEAD) / denominator.T[:, :, None]).reshape(
        rows, width
    )
    targets = layer_norm(attended).astype(jnp.bfloat16)
    blocks = target_mask.shape[1]
    groups = lax.axis_size("grp")
    capacity = max(2, (blocks + groups - 1) // groups)
    pred_size = pred_hidden.shape[2]
    owner_ids = owners[0, :, 0]
    live = target_mask[0]
    chosen = (
        (owner_ids[:, None] == jnp.arange(groups, dtype=jnp.int32)[None, :]) & (live[:, None] == 1)
    ).astype(jnp.int32)
    earlier = jnp.cumsum(chosen, axis=0) - chosen
    position = jnp.sum(earlier * chosen, axis=1)
    slot_index = owner_ids * capacity + position
    dispatch = (
        (jnp.arange(groups * capacity, dtype=jnp.int32)[:, None] == slot_index[None, :])
        & (live[None, :] == 1)
    ).astype(jnp.bfloat16)
    send_targets = (
        jnp.dot(dispatch, targets.reshape(blocks, 2 * width), preferred_element_type=jnp.float32)
        .astype(jnp.bfloat16)
        .reshape(groups, capacity, 2 * width)
    )
    send_hidden = (
        jnp.dot(
            dispatch,
            pred_hidden[0].reshape(blocks, 2 * pred_size),
            preferred_element_type=jnp.float32,
        )
        .astype(jnp.bfloat16)
        .reshape(groups, capacity, 2 * pred_size)
    )
    expert_weight = pred_weight[0]
    owner_grads = owner_compute(
        (
            lax.all_to_all(send_targets, "grp", split_axis=0, concat_axis=0, tiled=True),
            lax.all_to_all(send_hidden, "grp", split_axis=0, concat_axis=0, tiled=True),
        ),
        expert_weight,
    )
    back_grads = lax.all_to_all(owner_grads, "grp", split_axis=0, concat_axis=0, tiled=True)
    pair_grads = jnp.dot(
        dispatch.T,
        back_grads.reshape(groups * capacity, 2 * pred_size),
        preferred_element_type=jnp.float32,
    )
    pred_grad = pair_grads.astype(jnp.bfloat16).reshape(rows, pred_size)
    return (new_kv, targets[None], pred_grad[None])


LANES = 128
PAIR_BUDGET = 16 << 20
VM = pl.BlockSpec(memory_space=pltpu.VMEM)
HBM = pl.BlockSpec(memory_space=pltpu.HBM)


def local_call(body, outs, operands, specs=None, out_specs=None, cost=None, scratch=(), limit=4):
    return pl.pallas_call(
        body,
        out_shape=outs,
        in_specs=specs or [VM] * len(operands),
        out_specs=out_specs or jax.tree.map(lambda _: VM, outs),
        scratch_shapes=list(scratch),
        cost_estimate=cost,
        compiler_params=pltpu.CompilerParams(vmem_limit_bytes=limit << 20),
    )(*operands)


def shape_of(dims, kind=jnp.bfloat16):
    return jax.ShapeDtypeStruct(dims, kind)


def matmul_cost(rows, depth, columns, extra=0):
    return pl.CostEstimate(
        flops=2 * rows * depth * columns, bytes_accessed=2 * depth * columns, transcendentals=extra
    )


def chip_and_core():
    me = lax.axis_index("seq")
    return me // 2, lax.rem(me, 2)


def chip_tiles(tiles, is_first, with_values):
    lane = lax.broadcasted_iota(jnp.int32, tiles[0].shape, 1) < HEAD
    mixed = jnp.where(lane, tiles[5], tiles[2])
    first = [tiles[0], tiles[1], tiles[2]]
    second = [tiles[3], tiles[4], mixed]
    if with_values:
        first = first + tiles[5:8]
        second = second + tiles[8:11]
    own = [jnp.where(is_first, a, b) for a, b in zip(first, second)]
    other = [jnp.where(is_first, b, a) for a, b in zip(first, second)]
    return own, other


def norm_body(tokens, normed, keep, send):
    half = tokens.shape[1] // 2
    chip, _ = chip_and_core()
    values = layer_norm(tokens[...].astype(jnp.float32)).astype(jnp.bfloat16)
    normed[...] = values
    low, high = values[:, :half], values[:, half:]
    keep[...] = jnp.where(chip == 0, low, high)
    send[...] = jnp.where(chip == 0, high, low)


def split_product(rows, weight, own, other):
    chip, _ = chip_and_core()
    sums = jnp.dot(rows[...], weight[...], preferred_element_type=jnp.float32)
    tiles = [sums[:, t * LANES : (t + 1) * LANES] for t in range(sums.shape[1] // LANES)]
    mine, theirs = chip_tiles(tiles, chip == 0, True)
    for t in range(6):
        own[:, t * LANES : (t + 1) * LANES] = mine[t]
        other[:, t * LANES : (t + 1) * LANES] = theirs[t].astype(jnp.bfloat16)


def blend(target, context):
    return (
        keep_rate * target[...].astype(jnp.float32)
        + (1.0 - keep_rate) * context[...].astype(jnp.float32)
    ).astype(jnp.bfloat16)


def first_partial_body(
    target, context, other_target, other_context, rows, normed, query_weight,
    joined, own, q_own, send, stored, sem,
):
    chip, core = chip_and_core()
    depth = target.shape[0]
    own_rows = pl.ds(pl.multiple_of(core * depth, 16), depth)
    joined[own_rows, :] = blend(target, context)
    store = pltpu.make_async_copy(joined.at[own_rows], stored, sem)
    store.start()
    joined[pl.ds(pl.multiple_of((1 - core) * depth, 16), depth), :] = blend(
        other_target, other_context
    )
    split_product(rows, joined, own, send)
    queries = lax.dot_general(
        normed[...], query_weight[...], (((1,), (1,)), ((), ())), preferred_element_type=jnp.float32
    ).astype(jnp.bfloat16).astype(jnp.float32) * (1.0 / math.sqrt(HEAD))
    full = queries.shape[1] // LANES
    tiles = [queries[:, t * LANES : (t + 1) * LANES] for t in range(full)]
    rest = queries[:, full * LANES :]
    tiles.append(jnp.concatenate([rest, jnp.zeros_like(rest)], axis=1))
    mine, theirs = chip_tiles(tiles, chip == 0, False)
    for t in range(3):
        q_own[:, t * LANES : (t + 1) * LANES] = mine[t].astype(jnp.bfloat16)
        send[:, (6 + t) * LANES : (7 + t) * LANES] = theirs[t].astype(jnp.bfloat16)
    store.wait()


def partial_body(rows, weight, own, other):
    split_product(rows, weight, own, other)


def kv_body(own_sum, other_sum, from_other, received, q_own, kv, queries):
    rows, width = own_sum.shape
    kv[:rows, :] = (other_sum[...] + received[:, :width].astype(jnp.float32)).astype(kv.dtype)
    kv[rows:, :] = (own_sum[...] + from_other[...].astype(jnp.float32)).astype(kv.dtype)
    queries[:rows, :] = q_own[...]
    queries[rows:, :] = received[:, width:]


def add_keys(queries, kv_refs, slot):
    upper_lane = lax.broadcasted_iota(jnp.int32, (1, LANES), 1) >= HEAD
    tile, upper = slot // 2, slot % 2
    lane = upper_lane if upper else jnp.logical_not(upper_lane)
    q = queries[:, tile * LANES : (tile + 1) * LANES]
    q = jnp.where(lane, q, jnp.zeros_like(q))
    v_tile, v_upper = (slot + 1) % 6 // 2, (slot + 1) % 2
    v_lane = upper_lane if v_upper else jnp.logical_not(upper_lane)
    total = None
    for kv in kv_refs:
        keys = kv[:, tile * LANES : (tile + 1) * LANES]
        scores = lax.dot_general(
            q, keys, (((1,), (1,)), ((), ())), preferred_element_type=jnp.float32
        )
        weights = jnp.exp(scores).astype(jnp.bfloat16)
        start = (3 + v_tile) * LANES
        values = kv[:, start : start + LANES]
        values = jnp.where(v_lane, values, jnp.ones_like(values))
        part = jnp.dot(weights, values, preferred_element_type=jnp.float32)
        total = part if total is None else total + part
    return total


def attend_body(queries, kv_a, kv_b, mine, theirs):
    upper_lane = lax.broadcasted_iota(jnp.int32, (1, LANES), 1) >= HEAD
    rows = mine.shape[0]
    found = [None] * 6
    for slot in range(6):
        total = add_keys(queries, (kv_a, kv_b), slot)
        found[(slot + 1) % 6] = total / pltpu.roll(total, HEAD, 1)
    for t in range(3):
        joined = jnp.where(upper_lane, found[2 * t + 1], found[2 * t])
        mine[:, t * LANES : (t + 1) * LANES] = joined[:rows]
        theirs[:, t * LANES : (t + 1) * LANES] = joined[rows:].astype(theirs.dtype)


def match_body(match):
    token = lax.broadcasted_iota(jnp.int32, match.shape, 0) // 2
    pair = lax.broadcasted_iota(jnp.int32, match.shape, 1)
    match[...] = (token == pair).astype(match.dtype)


def token_values(match, pairs):
    return jnp.sum(match[...] * pairs[...], axis=1, keepdims=True)


def owner_at(moved, groups):
    me = lax.axis_index("grp")
    place = jnp.where(lax.rem(me, 2) == 0, me // 2, groups - 1 - me // 2)
    place = lax.rem(place + moved + groups, groups)
    return jnp.where(place < groups // 2, 2 * place, 2 * (groups - 1 - place) + 1)


def slot_owners(groups):
    _, core = chip_and_core()
    sign = 2 * core - 1
    owners = [owner_at(0, groups)]
    for step in range(1, groups // 2):
        owners += [owner_at(sign * step, groups), owner_at(-sign * step, groups)]
    return owners + [owner_at(groups // 2, groups)]


def join_halves(mine, theirs, joined):
    _, core = chip_and_core()
    rows = mine.shape[0]
    joined[pl.ds(pl.multiple_of(core * rows, 16), rows), :] = mine[...]
    joined[pl.ds(pl.multiple_of((1 - core) * rows, 16), rows), :] = theirs[...]


def add_predictions(match, owners, hidden, weights, ids_of):
    normed = layer_norm(hidden[...].astype(jnp.float32)).astype(jnp.bfloat16)
    ids = token_values(match, owners)
    total = None
    for weight, owner in zip(weights, ids_of):
        picked = jnp.where(ids == owner, normed, jnp.zeros_like(normed))
        part = lax.dot_general(
            picked, weight[...], (((1,), (1,)), ((), ())), preferred_element_type=jnp.float32
        )
        total = part if total is None else total + part
    return total


def predict_body(groups, match, owners, hidden, *refs):
    weights, prediction = refs[:-1], refs[-1]
    prediction[...] = add_predictions(match, owners, hidden, weights, slot_owners(groups))


def predict_rest_body(groups, match, owners, hidden, earlier, mine, theirs, *refs):
    weights, (prediction, joined) = refs[:-2], refs[-2:]
    join_halves(mine, theirs, joined)
    places = slot_owners(groups)[groups - 1 - len(weights) :]
    prediction[...] = earlier[...] + add_predictions(
        match, owners, hidden, (*weights, joined), places
    )


def cut_body(whole, first, second):
    _, core = chip_and_core()
    rows = first.shape[0]
    first[...] = whole[pl.ds(pl.multiple_of(core * rows, 16), rows), :]
    second[...] = whole[pl.ds(pl.multiple_of((1 - core) * rows, 16), rows), :]


def join_body(first, second, joined):
    join_halves(first, second, joined)


def add_upstream(residual, ids, weights, ids_of):
    total = None
    for weight, owner in zip(weights, ids_of):
        picked = jnp.where(ids == owner, residual, jnp.zeros_like(residual))
        part = jnp.dot(picked, weight[...], preferred_element_type=jnp.float32)
        total = part if total is None else total + part
    return total


def finish_body(groups, match, owners, mask, attended, returned, prediction, hidden, *refs):
    weights, (targets, grad) = refs[:-2], refs[-2:]
    chip, _ = chip_and_core()
    width, _ = targets.shape
    mine, theirs = attended[...], returned[...].astype(jnp.float32)
    joined = jnp.concatenate(
        [jnp.where(chip == 0, mine, theirs), jnp.where(chip == 0, theirs, mine)], axis=1
    )
    lane = lax.broadcasted_iota(jnp.int32, joined.shape, 1) >= HEAD
    joined = jnp.where(lane, joined, 0.0)
    mean = jnp.sum(joined, axis=1, keepdims=True) * (1.0 / width)
    center = jnp.where(lane, joined - mean, 0.0)
    variance = jnp.sum(center * center, axis=1, keepdims=True) * (1.0 / width)
    found = (center * lax.rsqrt(variance + epsilon))[:, HEAD:].astype(jnp.bfloat16)
    targets[...] = found.T
    residual = (prediction[...] - found.astype(jnp.float32)).astype(jnp.bfloat16)
    ids = token_values(match, owners)
    upstream = add_upstream(residual, ids, weights, slot_owners(groups))
    inputs = hidden[...].astype(jnp.float32)
    back = norm_backward(upstream, layer_norm(inputs), inputs)
    grad[...] = jnp.where(token_values(match, mask) == 1, back, 0.0).astype(grad.dtype)


def ring_pairs(members, groups):
    order = list(range(0, groups, 2)) + list(range(groups - 1, 0, -2))
    pairs = []
    for member in range(members):
        for i in range(groups):
            a, b = order[i], order[(i + 1) % groups]
            a, b = (a, b) if member % 2 == 0 else (b, a)
            pairs.append((member * groups + a, member * groups + b))
    return pairs


def paired_shards(
    tokens, target_kv, context_kv, query_weight, pred_hidden, pred_weight, target_mask, owners
):
    members = lax.axis_size("seq")
    groups = lax.axis_size("grp")
    across = [(i, (i + members // 2) % members) for i in range(members)]
    beside = [(i, i ^ 1) for i in range(members)]
    ring = ring_pairs(members, groups)
    rows, width = tokens.shape[1], query_weight.shape[0]
    features = tokens.shape[2]
    half = features // 2
    packed = 3 * LANES
    out_rows, pred_size = pred_weight.shape[1:]
    owner_row, mask_row = owners.reshape(1, -1), target_mask.reshape(1, -1)
    sums_shape = shape_of((rows, 2 * packed), jnp.float32)

    match = local_call(
        match_body,
        shape_of((rows, owner_row.shape[1]), jnp.int32),
        (),
    )
    other_target = lax.ppermute(target_kv, "seq", beside)
    other_context = lax.ppermute(context_kv, "seq", beside)
    normed, keep, send = local_call(
        norm_body,
        [shape_of((rows, features)), shape_of((rows, half)), shape_of((rows, half))],
        (tokens[0],),
        cost=pl.CostEstimate(flops=1 << 33, bytes_accessed=1 << 20, transcendentals=0),
    )
    kept_other = lax.ppermute(send, "seq", across)
    joined, own_sum, q_own, own_send, stored_kv = local_call(
        first_partial_body,
        [
            shape_of((half, 2 * width)),
            sums_shape,
            shape_of((rows, packed)),
            shape_of((rows, 3 * packed)),
            shape_of(target_kv.shape),
        ],
        (target_kv, context_kv, other_target, other_context, keep, normed, query_weight),
        out_specs=[VM] * 4 + [HBM],
        scratch=[pltpu.SemaphoreType.DMA],
        cost=matmul_cost(rows, half, 4 * width),
    )
    received = lax.ppermute(own_send, "seq", across)
    other_sum, other_send = local_call(
        partial_body,
        [sums_shape, shape_of((rows, 2 * packed))],
        (kept_other, joined),
        cost=matmul_cost(rows, half, 2 * width),
    )
    from_other = lax.ppermute(other_send, "seq", across)
    kv, queries = local_call(
        kv_body,
        [shape_of((2 * rows, 2 * packed)), shape_of((2 * rows, packed))],
        (own_sum, other_sum, from_other, received, q_own),
    )
    kv_beside = lax.ppermute(kv, "seq", beside)
    attended, send_back = local_call(
        attend_body,
        [shape_of((rows, packed), jnp.float32), shape_of((rows, packed))],
        (queries, kv, kv_beside),
        cost=matmul_cost(2 * rows, 12 * LANES, 4 * rows, 12 * rows * 4 * rows),
    )
    returned = lax.ppermute(send_back, "seq", across)

    half_rows = out_rows // 2
    half_shape, whole_shape = shape_of((half_rows, pred_size)), shape_of((out_rows, pred_size))
    halves = [half_shape, half_shape]
    weights = [pred_weight[0]]
    last_step = groups // 2
    for step in range(1, last_step):
        if step == 1:
            held = lax.ppermute(pred_weight[0], ("seq", "grp"), ring)
            first, second = local_call(cut_body, halves, (held,))
        else:
            first = lax.ppermute(first, ("seq", "grp"), ring)
            second = lax.ppermute(second, ("seq", "grp"), ring)
            held = local_call(join_body, whole_shape, (first, second))
        weights += [held, lax.ppermute(held, "seq", beside)]
    if last_step == 1:
        first, second = local_call(cut_body, halves, (pred_weight[0],))
    mine = lax.ppermute(first, ("seq", "grp"), ring)
    theirs = lax.ppermute(mine, "seq", beside)
    early = groups - 3 if groups > 4 else 1
    prediction = local_call(
        functools.partial(predict_body, groups),
        shape_of((rows, width), jnp.float32),
        (match, owner_row, pred_hidden[0], *weights[:early]),
        cost=matmul_cost(rows, early * pred_size, width),
    )
    prediction, opposite = local_call(
        functools.partial(predict_rest_body, groups),
        [shape_of((rows, width), jnp.float32), whole_shape],
        (match, owner_row, pred_hidden[0], prediction, mine, theirs, *weights[early:]),
        cost=matmul_cost(rows, (groups - early) * pred_size, width),
    )
    weights.append(opposite)
    targets, grad = local_call(
        functools.partial(finish_body, groups),
        [shape_of((width, rows)), shape_of((rows, pred_size))],
        (
            match, owner_row, mask_row, attended, returned, prediction, pred_hidden[0], *weights
        ),
        out_specs=[pl.BlockSpec(), pl.BlockSpec()],
        cost=matmul_cost(rows, groups * pred_size, width),
    )
    return (stored_kv, targets.T[None], grad[None])


def shards(*arguments):
    pred_weight = arguments[5]
    gathered = lax.axis_size("grp") * pred_weight.size * pred_weight.dtype.itemsize
    two_chips = lax.axis_size("seq") == 4
    if two_chips and lax.axis_size("grp") % 2 == 0 and gathered <= PAIR_BUDGET:
        return paired_shards(*arguments)
    return general_shards(*arguments)


def solution(mesh):
    placed = (
        P("grp", "seq", None),
        P("seq", None),
        P("seq", None),
        P(),
        P("grp", "seq", None),
        P("grp", None, None),
        P("grp", "seq"),
        P("grp", "seq", None),
    )
    return jax.shard_map(
        shards,
        mesh=mesh,
        in_specs=placed,
        out_specs=(P("seq", None), P("grp", "seq", None), P("grp", "seq", None)),
        check_vma=False,
    )
```

```python
import functools
import math

import jax
import jax.numpy as jnp
from jax import lax
from jax.experimental import pallas as pl
from jax.experimental.pallas import tpu as pltpu
from jax.sharding import PartitionSpec as P


HEAD = 64
HEADS = 11


keep_rate = 0.9
epsilon = 1e-05


def layer_norm(values):
    center = values - jnp.mean(values, axis=-1, keepdims=True)
    variance = jnp.mean(center * center, axis=-1, keepdims=True)
    return center * lax.rsqrt(variance + epsilon)


def norm_backward(upstream, normed, inputs):
    center = inputs - jnp.mean(inputs, axis=-1, keepdims=True)
    variance = jnp.mean(center * center, axis=-1, keepdims=True)
    inverse = lax.rsqrt(variance + epsilon)
    upstream_mean = jnp.mean(upstream, axis=-1, keepdims=True)
    cross_mean = jnp.mean(upstream * normed, axis=-1, keepdims=True)
    return inverse * (upstream - upstream_mean - normed * cross_mean)


def owner_compute(received, expert_weight):
    received_targets, received_hidden = received
    groups = received_targets.shape[0]
    items = received_targets.shape[1]
    pred_size = expert_weight.shape[1]
    width = expert_weight.shape[0]
    inputs = received_hidden.reshape(-1, pred_size).astype(jnp.float32)
    normed = layer_norm(inputs)
    prediction = jnp.einsum(
        "tp,ap->ta", normed.astype(jnp.bfloat16), expert_weight, preferred_element_type=jnp.float32
    )
    residual = prediction - received_targets.reshape(-1, width).astype(jnp.float32)
    upstream = jnp.dot(
        residual.astype(jnp.bfloat16), expert_weight, preferred_element_type=jnp.float32
    )
    grad = norm_backward(upstream, normed, inputs).astype(jnp.bfloat16)
    return grad.reshape(groups, items, 2 * pred_size)


def general_shards(
    tokens, target_kv, context_kv, query_weight, pred_hidden, pred_weight, target_mask, owners
):
    new_kv = (
        keep_rate * target_kv.astype(jnp.float32)
        + (1.0 - keep_rate) * context_kv.astype(jnp.float32)
    ).astype(jnp.bfloat16)
    width = HEADS * HEAD
    scale = 1.0 / math.sqrt(HEAD)
    rows = tokens.shape[1]
    normed = layer_norm(tokens[0].astype(jnp.float32)).astype(jnp.bfloat16)
    queries = jnp.einsum(
        "td,ad->ta", normed, query_weight, preferred_element_type=jnp.float32
    ).astype(jnp.bfloat16)
    query_heads = queries.reshape(rows, HEADS, HEAD)
    own_kv = jnp.dot(
        normed,
        lax.all_gather(new_kv, "seq", axis=0, tiled=True),
        preferred_element_type=jnp.float32,
    ).astype(jnp.bfloat16)
    key_values = lax.all_gather(own_kv, "seq", axis=0, tiled=True)
    count = key_values.shape[0]
    keys = key_values[:, :width].reshape(count, HEADS, HEAD)
    values = key_values[:, width:].reshape(count, HEADS, HEAD)
    scores = (
        jnp.einsum("qhd,khd->hqk", query_heads, keys, preferred_element_type=jnp.float32) * scale
    )
    expo = jnp.exp(scores)
    added = jnp.einsum(
        "hqk,khd->qhd", expo.astype(jnp.bfloat16), values, preferred_element_type=jnp.float32
    )
    numerator = added.reshape(rows, width)
    denominator = jnp.sum(expo, axis=-1)
    attended = (numerator.reshape(rows, HEADS, HEAD) / denominator.T[:, :, None]).reshape(
        rows, width
    )
    targets = layer_norm(attended).astype(jnp.bfloat16)
    blocks = target_mask.shape[1]
    groups = lax.axis_size("grp")
    capacity = max(2, (blocks + groups - 1) // groups)
    pred_size = pred_hidden.shape[2]
    owner_ids = owners[0, :, 0]
    live = target_mask[0]
    chosen = (
        (owner_ids[:, None] == jnp.arange(groups, dtype=jnp.int32)[None, :]) & (live[:, None] == 1)
    ).astype(jnp.int32)
    earlier = jnp.cumsum(chosen, axis=0) - chosen
    position = jnp.sum(earlier * chosen, axis=1)
    slot_index = owner_ids * capacity + position
    dispatch = (
        (jnp.arange(groups * capacity, dtype=jnp.int32)[:, None] == slot_index[None, :])
        & (live[None, :] == 1)
    ).astype(jnp.bfloat16)
    send_targets = (
        jnp.dot(dispatch, targets.reshape(blocks, 2 * width), preferred_element_type=jnp.float32)
        .astype(jnp.bfloat16)
        .reshape(groups, capacity, 2 * width)
    )
    send_hidden = (
        jnp.dot(
            dispatch,
            pred_hidden[0].reshape(blocks, 2 * pred_size),
            preferred_element_type=jnp.float32,
        )
        .astype(jnp.bfloat16)
        .reshape(groups, capacity, 2 * pred_size)
    )
    expert_weight = pred_weight[0]
    owner_grads = owner_compute(
        (
            lax.all_to_all(send_targets, "grp", split_axis=0, concat_axis=0, tiled=True),
            lax.all_to_all(send_hidden, "grp", split_axis=0, concat_axis=0, tiled=True),
        ),
        expert_weight,
    )
    back_grads = lax.all_to_all(owner_grads, "grp", split_axis=0, concat_axis=0, tiled=True)
    pair_grads = jnp.dot(
        dispatch.T,
        back_grads.reshape(groups * capacity, 2 * pred_size),
        preferred_element_type=jnp.float32,
    )
    pred_grad = pair_grads.astype(jnp.bfloat16).reshape(rows, pred_size)
    return (new_kv, targets[None], pred_grad[None])


LANES = 128
PAIR_BUDGET = 16 << 20
VM = pl.BlockSpec(memory_space=pltpu.VMEM)
HBM = pl.BlockSpec(memory_space=pltpu.HBM)


def local_call(body, outs, operands, specs=None, out_specs=None, cost=None, scratch=(), limit=4):
    return pl.pallas_call(
        body,
        out_shape=outs,
        in_specs=specs or [VM] * len(operands),
        out_specs=out_specs or jax.tree.map(lambda _: VM, outs),
        scratch_shapes=list(scratch),
        cost_estimate=cost,
        compiler_params=pltpu.CompilerParams(vmem_limit_bytes=limit << 20),
    )(*operands)


def shape_of(dims, kind=jnp.bfloat16):
    return jax.ShapeDtypeStruct(dims, kind)


def matmul_cost(rows, depth, columns, extra=0):
    return pl.CostEstimate(
        flops=2 * rows * depth * columns, bytes_accessed=2 * depth * columns, transcendentals=extra
    )


def chip_and_core():
    me = lax.axis_index("seq")
    return me // 2, lax.rem(me, 2)


def chip_tiles(tiles, is_first, with_values):
    lane = lax.broadcasted_iota(jnp.int32, tiles[0].shape, 1) < HEAD
    mixed = jnp.where(lane, tiles[5], tiles[2])
    first = [tiles[0], tiles[1], tiles[2]]
    second = [tiles[3], tiles[4], mixed]
    if with_values:
        first = first + tiles[5:8]
        second = second + tiles[8:11]
    own = [jnp.where(is_first, a, b) for a, b in zip(first, second)]
    other = [jnp.where(is_first, b, a) for a, b in zip(first, second)]
    return own, other


def norm_body(tokens, normed, keep, send):
    half = tokens.shape[1] // 2
    chip, _ = chip_and_core()
    values = layer_norm(tokens[...].astype(jnp.float32)).astype(jnp.bfloat16)
    normed[...] = values
    low, high = values[:, :half], values[:, half:]
    keep[...] = jnp.where(chip == 0, low, high)
    send[...] = jnp.where(chip == 0, high, low)


def split_product(rows, weight, own, other):
    chip, _ = chip_and_core()
    sums = jnp.dot(rows[...], weight[...], preferred_element_type=jnp.float32)
    tiles = [sums[:, t * LANES : (t + 1) * LANES] for t in range(sums.shape[1] // LANES)]
    mine, theirs = chip_tiles(tiles, chip == 0, True)
    for t in range(6):
        own[:, t * LANES : (t + 1) * LANES] = mine[t]
        other[:, t * LANES : (t + 1) * LANES] = theirs[t].astype(jnp.bfloat16)


def blend(target, context):
    return (
        keep_rate * target[...].astype(jnp.float32)
        + (1.0 - keep_rate) * context[...].astype(jnp.float32)
    ).astype(jnp.bfloat16)


def first_partial_body(
    target, context, other_target, other_context, rows, normed, query_weight,
    joined, own, q_own, send, stored, sem,
):
    chip, core = chip_and_core()
    depth = target.shape[0]
    own_rows = pl.ds(pl.multiple_of(core * depth, 16), depth)
    joined[own_rows, :] = blend(target, context)
    joined[pl.ds(pl.multiple_of((1 - core) * depth, 16), depth), :] = blend(
        other_target, other_context
    )
    store = pltpu.make_async_copy(joined.at[own_rows], stored, sem)
    store.start()
    split_product(rows, joined, own, send)
    queries = lax.dot_general(
        normed[...], query_weight[...], (((1,), (1,)), ((), ())), preferred_element_type=jnp.float32
    ).astype(jnp.bfloat16).astype(jnp.float32) * (1.0 / math.sqrt(HEAD))
    full = queries.shape[1] // LANES
    tiles = [queries[:, t * LANES : (t + 1) * LANES] for t in range(full)]
    rest = queries[:, full * LANES :]
    tiles.append(jnp.concatenate([rest, jnp.zeros_like(rest)], axis=1))
    mine, theirs = chip_tiles(tiles, chip == 0, False)
    for t in range(3):
        q_own[:, t * LANES : (t + 1) * LANES] = mine[t].astype(jnp.bfloat16)
        send[:, (6 + t) * LANES : (7 + t) * LANES] = theirs[t].astype(jnp.bfloat16)
    store.wait()


def partial_body(rows, weight, own, other):
    split_product(rows, weight, own, other)


def kv_body(own_sum, other_sum, from_other, received, q_own, kv, queries):
    rows, width = own_sum.shape
    kv[:rows, :] = (other_sum[...] + received[:, :width].astype(jnp.float32)).astype(kv.dtype)
    kv[rows:, :] = (own_sum[...] + from_other[...].astype(jnp.float32)).astype(kv.dtype)
    queries[:rows, :] = q_own[...]
    queries[rows:, :] = received[:, width:]


def add_keys(queries, kv_refs, slot):
    upper_lane = lax.broadcasted_iota(jnp.int32, (1, LANES), 1) >= HEAD
    tile, upper = slot // 2, slot % 2
    lane = upper_lane if upper else jnp.logical_not(upper_lane)
    q = queries[:, tile * LANES : (tile + 1) * LANES]
    q = jnp.where(lane, q, jnp.zeros_like(q))
    v_tile, v_upper = (slot + 1) % 6 // 2, (slot + 1) % 2
    v_lane = upper_lane if v_upper else jnp.logical_not(upper_lane)
    total = None
    for kv in kv_refs:
        keys = kv[:, tile * LANES : (tile + 1) * LANES]
        scores = lax.dot_general(
            q, keys, (((1,), (1,)), ((), ())), preferred_element_type=jnp.float32
        )
        weights = jnp.exp(scores).astype(jnp.bfloat16)
        start = (3 + v_tile) * LANES
        values = kv[:, start : start + LANES]
        values = jnp.where(v_lane, values, jnp.ones_like(values))
        part = jnp.dot(weights, values, preferred_element_type=jnp.float32)
        total = part if total is None else total + part
    return total


def attend_body(queries, kv_a, kv_b, mine, theirs):
    upper_lane = lax.broadcasted_iota(jnp.int32, (1, LANES), 1) >= HEAD
    rows = mine.shape[0]
    for t in range(3):
        low = add_keys(queries, (kv_a, kv_b), (2 * t + 5) % 6)
        high = add_keys(queries, (kv_a, kv_b), 2 * t)
        sums = pltpu.roll(jnp.where(upper_lane, low, high), HEAD, 1)
        joined = jnp.where(upper_lane, high, low) / sums
        mine[:, t * LANES : (t + 1) * LANES] = joined[:rows]
        theirs[:, t * LANES : (t + 1) * LANES] = joined[rows:].astype(theirs.dtype)


def token_values(pairs, rows):
    shape = (rows, pairs.shape[1])
    token = lax.broadcasted_iota(jnp.int32, shape, 0) // 2
    pair = lax.broadcasted_iota(jnp.int32, shape, 1)
    return jnp.sum(jnp.where(token == pair, pairs[...], 0), axis=1, keepdims=True)


def hidden_body(owners, mask, hidden, normed, factor, ids):
    inputs = hidden[...].astype(jnp.float32)
    rows = inputs.shape[0]
    center = inputs - jnp.mean(inputs, axis=-1, keepdims=True)
    inverse = lax.rsqrt(jnp.mean(center * center, axis=-1, keepdims=True) + epsilon)
    normed[...] = center * inverse
    live = token_values(mask, rows) == 1
    factor[...] = jnp.broadcast_to(jnp.where(live, inverse, 0.0), factor.shape)
    ids[...] = jnp.broadcast_to(token_values(owners, rows), ids.shape)


def owner_at(moved, groups):
    me = lax.axis_index("grp")
    place = jnp.where(lax.rem(me, 2) == 0, me // 2, groups - 1 - me // 2)
    place = lax.rem(place + moved + groups, groups)
    return jnp.where(place < groups // 2, 2 * place, 2 * (groups - 1 - place) + 1)


def slot_owners(groups):
    _, core = chip_and_core()
    sign = 2 * core - 1
    owners = [owner_at(0, groups)]
    for step in range(1, groups // 2):
        owners += [owner_at(sign * step, groups), owner_at(-sign * step, groups)]
    return owners + [owner_at(groups // 2, groups)]


def join_halves(mine, theirs, joined):
    _, core = chip_and_core()
    rows = mine.shape[0]
    joined[pl.ds(pl.multiple_of(core * rows, 16), rows), :] = mine[...]
    joined[pl.ds(pl.multiple_of((1 - core) * rows, 16), rows), :] = theirs[...]


def add_predictions(ids, normed, weights, ids_of):
    values, owner_of = normed[...].astype(jnp.bfloat16), ids[:, :1]
    total = None
    for weight, owner in zip(weights, ids_of):
        picked = jnp.where(owner_of == owner, values, jnp.zeros_like(values))
        part = lax.dot_general(
            picked, weight[...], (((1,), (1,)), ((), ())), preferred_element_type=jnp.float32
        )
        total = part if total is None else total + part
    return total


def predict_body(groups, ids, normed, *refs):
    weights, prediction = refs[:-1], refs[-1]
    prediction[...] = add_predictions(ids, normed, weights, slot_owners(groups))


def predict_more_body(groups, done, ids, normed, earlier, *refs):
    weights, prediction = refs[:-1], refs[-1]
    places = slot_owners(groups)[done : done + len(weights)]
    prediction[...] = earlier[...] + add_predictions(ids, normed, weights, places)


def predict_rest_body(groups, ids, normed, earlier, mine, theirs, *refs):
    weights, (prediction, joined) = refs[:-2], refs[-2:]
    join_halves(mine, theirs, joined)
    places = slot_owners(groups)[groups - 1 - len(weights) :]
    prediction[...] = earlier[...] + add_predictions(ids, normed, (*weights, joined), places)


def cut_body(whole, first, second):
    _, core = chip_and_core()
    rows = first.shape[0]
    first[...] = whole[pl.ds(pl.multiple_of(core * rows, 16), rows), :]
    second[...] = whole[pl.ds(pl.multiple_of((1 - core) * rows, 16), rows), :]


def join_body(first, second, joined):
    join_halves(first, second, joined)


def pick_upstream(residual, ids, weights, ids_of):
    owner_of = jnp.tile(ids[...], (1, weights[0].shape[1] // ids.shape[1]))
    total = None
    for weight, owner in zip(weights, ids_of):
        part = jnp.dot(residual, weight[...], preferred_element_type=jnp.float32)
        total = part if total is None else jnp.where(owner_of == owner, part, total)
    return total


def finish_body(groups, ids, normed, factor, attended, returned, prediction, *refs):
    weights, (targets, grad) = refs[:-2], refs[-2:]
    chip, _ = chip_and_core()
    width, _ = targets.shape
    mine, theirs = attended[...], returned[...].astype(jnp.float32)
    joined = jnp.concatenate(
        [jnp.where(chip == 0, mine, theirs), jnp.where(chip == 0, theirs, mine)], axis=1
    )
    lane = lax.broadcasted_iota(jnp.int32, joined.shape, 1) >= HEAD
    joined = jnp.where(lane, joined, 0.0)
    mean = jnp.sum(joined, axis=1, keepdims=True) * (1.0 / width)
    center = jnp.where(lane, joined - mean, 0.0)
    variance = jnp.sum(center * center, axis=1, keepdims=True) * (1.0 / width)
    found = (center * lax.rsqrt(variance + epsilon))[:, HEAD:].astype(jnp.bfloat16)
    targets[...] = found.T
    residual = (prediction[...] - found.astype(jnp.float32)).astype(jnp.bfloat16)
    upstream = pick_upstream(residual, ids, weights, slot_owners(groups))
    values = normed[...]
    mean = jnp.mean(upstream, axis=-1, keepdims=True)
    cross = jnp.mean(upstream * values, axis=-1, keepdims=True)
    scale = jnp.tile(factor[...], (1, values.shape[1] // factor.shape[1]))
    grad[...] = (scale * (upstream - mean - values * cross)).astype(grad.dtype)


def ring_pairs(members, groups):
    order = list(range(0, groups, 2)) + list(range(groups - 1, 0, -2))
    pairs = []
    for member in range(members):
        for i in range(groups):
            a, b = order[i], order[(i + 1) % groups]
            a, b = (a, b) if member % 2 == 0 else (b, a)
            pairs.append((member * groups + a, member * groups + b))
    return pairs


def paired_shards(
    tokens, target_kv, context_kv, query_weight, pred_hidden, pred_weight, target_mask, owners
):
    members = lax.axis_size("seq")
    groups = lax.axis_size("grp")
    across = [(i, (i + members // 2) % members) for i in range(members)]
    beside = [(i, i ^ 1) for i in range(members)]
    ring = ring_pairs(members, groups)
    rows, width = tokens.shape[1], query_weight.shape[0]
    features = tokens.shape[2]
    half = features // 2
    packed = 3 * LANES
    out_rows, pred_size = pred_weight.shape[1:]
    owner_row, mask_row = owners.reshape(1, -1), target_mask.reshape(1, -1)
    sums_shape = shape_of((rows, 2 * packed), jnp.float32)

    other_target = lax.ppermute(target_kv, "seq", beside)
    other_context = lax.ppermute(context_kv, "seq", beside)
    normed, keep, send = local_call(
        norm_body,
        [shape_of((rows, features)), shape_of((rows, half)), shape_of((rows, half))],
        (tokens[0],),
        cost=pl.CostEstimate(flops=1 << 33, bytes_accessed=1 << 20, transcendentals=0),
    )
    kept_other = lax.ppermute(send, "seq", across)
    joined, own_sum, q_own, own_send, stored_kv = local_call(
        first_partial_body,
        [
            shape_of((half, 2 * width)),
            sums_shape,
            shape_of((rows, packed)),
            shape_of((rows, 3 * packed)),
            shape_of(target_kv.shape),
        ],
        (target_kv, context_kv, other_target, other_context, keep, normed, query_weight),
        out_specs=[VM] * 4 + [HBM],
        scratch=[pltpu.SemaphoreType.DMA],
        cost=matmul_cost(rows, half, 4 * width),
    )
    received = lax.ppermute(own_send, "seq", across)
    other_sum, other_send = local_call(
        partial_body,
        [sums_shape, shape_of((rows, 2 * packed))],
        (kept_other, joined),
        cost=matmul_cost(rows, half, 2 * width),
    )
    from_other = lax.ppermute(other_send, "seq", across)
    kv, queries = local_call(
        kv_body,
        [shape_of((2 * rows, 2 * packed)), shape_of((2 * rows, packed))],
        (own_sum, other_sum, from_other, received, q_own),
    )
    kv_beside = lax.ppermute(kv, "seq", beside)
    attended, send_back = local_call(
        attend_body,
        [shape_of((rows, packed), jnp.float32), shape_of((rows, packed))],
        (queries, kv, kv_beside),
        cost=matmul_cost(2 * rows, 12 * LANES, 4 * rows, 12 * rows * 4 * rows),
    )
    returned = lax.ppermute(send_back, "seq", across)

    half_rows = out_rows // 2
    half_shape, whole_shape = shape_of((half_rows, pred_size)), shape_of((out_rows, pred_size))
    halves = [half_shape, half_shape]
    weights = [pred_weight[0]]
    last_step = groups // 2
    for step in range(1, last_step):
        if step == 1:
            held = lax.ppermute(pred_weight[0], ("seq", "grp"), ring)
            first, second = local_call(cut_body, halves, (held,))
        else:
            first = lax.ppermute(first, ("seq", "grp"), ring)
            second = lax.ppermute(second, ("seq", "grp"), ring)
            held = local_call(join_body, whole_shape, (first, second))
        weights += [held, lax.ppermute(held, "seq", beside)]
    if last_step == 1:
        first, second = local_call(cut_body, halves, (pred_weight[0],))
    mine = lax.ppermute(first, ("seq", "grp"), ring)
    theirs = lax.ppermute(mine, "seq", beside)
    early, most = min(3, groups - 1), groups - 1
    normed_hidden, factor, ids = local_call(
        hidden_body,
        [
            shape_of((rows, pred_size), jnp.float32),
            shape_of((rows, LANES), jnp.float32),
            shape_of((rows, LANES), jnp.int32),
        ],
        (owner_row, mask_row, pred_hidden[0]),
    )
    prediction = local_call(
        functools.partial(predict_body, groups),
        shape_of((rows, width), jnp.float32),
        (ids, normed_hidden, *weights[:early]),
        cost=matmul_cost(rows, early * pred_size, width),
    )
    if most > early:
        prediction = local_call(
            functools.partial(predict_more_body, groups, early),
            shape_of((rows, width), jnp.float32),
            (ids, normed_hidden, prediction, *weights[early:most]),
            cost=matmul_cost(rows, (most - early) * pred_size, width),
        )
    prediction, opposite = local_call(
        functools.partial(predict_rest_body, groups),
        [shape_of((rows, width), jnp.float32), whole_shape],
        (ids, normed_hidden, prediction, mine, theirs),
        cost=matmul_cost(rows, pred_size, width),
    )
    weights.append(opposite)
    targets, grad = local_call(
        functools.partial(finish_body, groups),
        [shape_of((width, rows)), shape_of((rows, pred_size))],
        (ids, normed_hidden, factor, attended, returned, prediction, *weights),
        out_specs=[pl.BlockSpec(), pl.BlockSpec()],
        cost=matmul_cost(rows, groups * pred_size, width),
    )
    return (stored_kv, targets.T[None], grad[None])


def shards(*arguments):
    pred_weight = arguments[5]
    gathered = lax.axis_size("grp") * pred_weight.size * pred_weight.dtype.itemsize
    two_chips = lax.axis_size("seq") == 4
    if two_chips and lax.axis_size("grp") % 2 == 0 and gathered <= PAIR_BUDGET:
        return paired_shards(*arguments)
    return general_shards(*arguments)


def solution(mesh):
    placed = (
        P("grp", "seq", None),
        P("seq", None),
        P("seq", None),
        P(),
        P("grp", "seq", None),
        P("grp", None, None),
        P("grp", "seq"),
        P("grp", "seq", None),
    )
    return jax.shard_map(
        shards,
        mesh=mesh,
        in_specs=placed,
        out_specs=(P("seq", None), P("grp", "seq", None), P("grp", "seq", None)),
        check_vma=False,
    )
```

```python
import functools
import math

import jax
import jax.numpy as jnp
from jax import lax
from jax.experimental import pallas as pl
from jax.experimental.pallas import tpu as pltpu
from jax.sharding import PartitionSpec as P


HEAD = 64
HEADS = 11


keep_rate = 0.9
epsilon = 1e-05


def layer_norm(values):
    center = values - jnp.mean(values, axis=-1, keepdims=True)
    variance = jnp.mean(center * center, axis=-1, keepdims=True)
    return center * lax.rsqrt(variance + epsilon)


def norm_backward(upstream, normed, inputs):
    center = inputs - jnp.mean(inputs, axis=-1, keepdims=True)
    variance = jnp.mean(center * center, axis=-1, keepdims=True)
    inverse = lax.rsqrt(variance + epsilon)
    upstream_mean = jnp.mean(upstream, axis=-1, keepdims=True)
    cross_mean = jnp.mean(upstream * normed, axis=-1, keepdims=True)
    return inverse * (upstream - upstream_mean - normed * cross_mean)


def owner_compute(received, expert_weight):
    received_targets, received_hidden = received
    groups = received_targets.shape[0]
    items = received_targets.shape[1]
    pred_size = expert_weight.shape[1]
    width = expert_weight.shape[0]
    inputs = received_hidden.reshape(-1, pred_size).astype(jnp.float32)
    normed = layer_norm(inputs)
    prediction = jnp.einsum(
        "tp,ap->ta", normed.astype(jnp.bfloat16), expert_weight, preferred_element_type=jnp.float32
    )
    residual = prediction - received_targets.reshape(-1, width).astype(jnp.float32)
    upstream = jnp.dot(
        residual.astype(jnp.bfloat16), expert_weight, preferred_element_type=jnp.float32
    )
    grad = norm_backward(upstream, normed, inputs).astype(jnp.bfloat16)
    return grad.reshape(groups, items, 2 * pred_size)


def general_shards(
    tokens, target_kv, context_kv, query_weight, pred_hidden, pred_weight, target_mask, owners
):
    new_kv = (
        keep_rate * target_kv.astype(jnp.float32)
        + (1.0 - keep_rate) * context_kv.astype(jnp.float32)
    ).astype(jnp.bfloat16)
    width = HEADS * HEAD
    scale = 1.0 / math.sqrt(HEAD)
    rows = tokens.shape[1]
    normed = layer_norm(tokens[0].astype(jnp.float32)).astype(jnp.bfloat16)
    queries = jnp.einsum(
        "td,ad->ta", normed, query_weight, preferred_element_type=jnp.float32
    ).astype(jnp.bfloat16)
    query_heads = queries.reshape(rows, HEADS, HEAD)
    own_kv = jnp.dot(
        normed,
        lax.all_gather(new_kv, "seq", axis=0, tiled=True),
        preferred_element_type=jnp.float32,
    ).astype(jnp.bfloat16)
    key_values = lax.all_gather(own_kv, "seq", axis=0, tiled=True)
    count = key_values.shape[0]
    keys = key_values[:, :width].reshape(count, HEADS, HEAD)
    values = key_values[:, width:].reshape(count, HEADS, HEAD)
    scores = (
        jnp.einsum("qhd,khd->hqk", query_heads, keys, preferred_element_type=jnp.float32) * scale
    )
    expo = jnp.exp(scores)
    added = jnp.einsum(
        "hqk,khd->qhd", expo.astype(jnp.bfloat16), values, preferred_element_type=jnp.float32
    )
    numerator = added.reshape(rows, width)
    denominator = jnp.sum(expo, axis=-1)
    attended = (numerator.reshape(rows, HEADS, HEAD) / denominator.T[:, :, None]).reshape(
        rows, width
    )
    targets = layer_norm(attended).astype(jnp.bfloat16)
    blocks = target_mask.shape[1]
    groups = lax.axis_size("grp")
    capacity = max(2, (blocks + groups - 1) // groups)
    pred_size = pred_hidden.shape[2]
    owner_ids = owners[0, :, 0]
    live = target_mask[0]
    chosen = (
        (owner_ids[:, None] == jnp.arange(groups, dtype=jnp.int32)[None, :]) & (live[:, None] == 1)
    ).astype(jnp.int32)
    earlier = jnp.cumsum(chosen, axis=0) - chosen
    position = jnp.sum(earlier * chosen, axis=1)
    slot_index = owner_ids * capacity + position
    dispatch = (
        (jnp.arange(groups * capacity, dtype=jnp.int32)[:, None] == slot_index[None, :])
        & (live[None, :] == 1)
    ).astype(jnp.bfloat16)
    send_targets = (
        jnp.dot(dispatch, targets.reshape(blocks, 2 * width), preferred_element_type=jnp.float32)
        .astype(jnp.bfloat16)
        .reshape(groups, capacity, 2 * width)
    )
    send_hidden = (
        jnp.dot(
            dispatch,
            pred_hidden[0].reshape(blocks, 2 * pred_size),
            preferred_element_type=jnp.float32,
        )
        .astype(jnp.bfloat16)
        .reshape(groups, capacity, 2 * pred_size)
    )
    expert_weight = pred_weight[0]
    owner_grads = owner_compute(
        (
            lax.all_to_all(send_targets, "grp", split_axis=0, concat_axis=0, tiled=True),
            lax.all_to_all(send_hidden, "grp", split_axis=0, concat_axis=0, tiled=True),
        ),
        expert_weight,
    )
    back_grads = lax.all_to_all(owner_grads, "grp", split_axis=0, concat_axis=0, tiled=True)
    pair_grads = jnp.dot(
        dispatch.T,
        back_grads.reshape(groups * capacity, 2 * pred_size),
        preferred_element_type=jnp.float32,
    )
    pred_grad = pair_grads.astype(jnp.bfloat16).reshape(rows, pred_size)
    return (new_kv, targets[None], pred_grad[None])


LANES = 128
PAIR_BUDGET = 16 << 20
VM = pl.BlockSpec(memory_space=pltpu.VMEM)
HBM = pl.BlockSpec(memory_space=pltpu.HBM)


def local_call(body, outs, operands, specs=None, out_specs=None, cost=None, scratch=(), limit=4):
    return pl.pallas_call(
        body,
        out_shape=outs,
        in_specs=specs or [VM] * len(operands),
        out_specs=out_specs or jax.tree.map(lambda _: VM, outs),
        scratch_shapes=list(scratch),
        cost_estimate=cost,
        compiler_params=pltpu.CompilerParams(vmem_limit_bytes=limit << 20),
    )(*operands)


def shape_of(dims, kind=jnp.bfloat16):
    return jax.ShapeDtypeStruct(dims, kind)


def matmul_cost(rows, depth, columns, extra=0):
    return pl.CostEstimate(
        flops=2 * rows * depth * columns, bytes_accessed=2 * depth * columns, transcendentals=extra
    )


def chip_and_core():
    me = lax.axis_index("seq")
    return me // 2, lax.rem(me, 2)


def chip_tiles(tiles, is_first, with_values):
    lane = lax.broadcasted_iota(jnp.int32, tiles[0].shape, 1) < HEAD
    mixed = jnp.where(lane, tiles[5], tiles[2])
    first = [tiles[0], tiles[1], tiles[2]]
    second = [tiles[3], tiles[4], mixed]
    if with_values:
        first = first + tiles[5:8]
        second = second + tiles[8:11]
    own = [jnp.where(is_first, a, b) for a, b in zip(first, second)]
    other = [jnp.where(is_first, b, a) for a, b in zip(first, second)]
    return own, other


def norm_body(tokens, normed, keep, send):
    half = tokens.shape[1] // 2
    chip, _ = chip_and_core()
    values = layer_norm(tokens[...].astype(jnp.float32)).astype(jnp.bfloat16)
    normed[...] = values
    low, high = values[:, :half], values[:, half:]
    keep[...] = jnp.where(chip == 0, low, high)
    send[...] = jnp.where(chip == 0, high, low)


def split_product(rows, weight, own, other):
    chip, _ = chip_and_core()
    sums = jnp.dot(rows[...], weight[...], preferred_element_type=jnp.float32)
    tiles = [sums[:, t * LANES : (t + 1) * LANES] for t in range(sums.shape[1] // LANES)]
    mine, theirs = chip_tiles(tiles, chip == 0, True)
    for t in range(6):
        own[:, t * LANES : (t + 1) * LANES] = mine[t]
        other[:, t * LANES : (t + 1) * LANES] = theirs[t].astype(jnp.bfloat16)


def first_partial_body(
    own_weight, other_weight, rows, normed, query_weight, joined, own, q_own, send, stored, sem
):
    chip, core = chip_and_core()
    depth = own_weight.shape[0]
    store = pltpu.make_async_copy(own_weight, stored, sem)
    store.start()
    joined[pl.ds(pl.multiple_of(core * depth, 16), depth), :] = own_weight[...]
    joined[pl.ds(pl.multiple_of((1 - core) * depth, 16), depth), :] = other_weight[...]
    split_product(rows, joined, own, send)
    queries = lax.dot_general(
        normed[...], query_weight[...], (((1,), (1,)), ((), ())), preferred_element_type=jnp.float32
    ).astype(jnp.bfloat16).astype(jnp.float32) * (1.0 / math.sqrt(HEAD))
    full = queries.shape[1] // LANES
    tiles = [queries[:, t * LANES : (t + 1) * LANES] for t in range(full)]
    rest = queries[:, full * LANES :]
    tiles.append(jnp.concatenate([rest, jnp.zeros_like(rest)], axis=1))
    mine, theirs = chip_tiles(tiles, chip == 0, False)
    for t in range(3):
        q_own[:, t * LANES : (t + 1) * LANES] = mine[t].astype(jnp.bfloat16)
        send[:, (6 + t) * LANES : (7 + t) * LANES] = theirs[t].astype(jnp.bfloat16)
    store.wait()


def partial_body(rows, weight, own, other):
    split_product(rows, weight, own, other)


def kv_body(own_sum, other_sum, from_other, received, q_own, kv, queries):
    rows, width = own_sum.shape
    kv[:rows, :] = (other_sum[...] + received[:, :width].astype(jnp.float32)).astype(kv.dtype)
    kv[rows:, :] = (own_sum[...] + from_other[...].astype(jnp.float32)).astype(kv.dtype)
    queries[:rows, :] = q_own[...]
    queries[rows:, :] = received[:, width:]


def add_keys(queries, kv_refs, slot):
    upper_lane = lax.broadcasted_iota(jnp.int32, (1, LANES), 1) >= HEAD
    tile, upper = slot // 2, slot % 2
    lane = upper_lane if upper else jnp.logical_not(upper_lane)
    q = queries[:, tile * LANES : (tile + 1) * LANES]
    q = jnp.where(lane, q, jnp.zeros_like(q))
    v_tile, v_upper = (slot + 1) % 6 // 2, (slot + 1) % 2
    v_lane = upper_lane if v_upper else jnp.logical_not(upper_lane)
    total = None
    for kv in kv_refs:
        keys = kv[:, tile * LANES : (tile + 1) * LANES]
        scores = lax.dot_general(
            q, keys, (((1,), (1,)), ((), ())), preferred_element_type=jnp.float32
        )
        weights = jnp.exp(scores).astype(jnp.bfloat16)
        start = (3 + v_tile) * LANES
        values = kv[:, start : start + LANES]
        values = jnp.where(v_lane, values, jnp.ones_like(values))
        part = jnp.dot(weights, values, preferred_element_type=jnp.float32)
        total = part if total is None else total + part
    return total


def attend_body(queries, kv_a, kv_b, mine, theirs):
    upper_lane = lax.broadcasted_iota(jnp.int32, (1, LANES), 1) >= HEAD
    rows = mine.shape[0]
    for t in range(3):
        low = add_keys(queries, (kv_a, kv_b), (2 * t + 5) % 6)
        high = add_keys(queries, (kv_a, kv_b), 2 * t)
        sums = pltpu.roll(jnp.where(upper_lane, low, high), HEAD, 1)
        joined = jnp.where(upper_lane, high, low) / sums
        mine[:, t * LANES : (t + 1) * LANES] = joined[:rows]
        theirs[:, t * LANES : (t + 1) * LANES] = joined[rows:].astype(theirs.dtype)


def token_values(pairs, rows):
    shape = (rows, pairs.shape[1])
    token = lax.broadcasted_iota(jnp.int32, shape, 0) // 2
    pair = lax.broadcasted_iota(jnp.int32, shape, 1)
    return jnp.sum(jnp.where(token == pair, pairs[...], 0), axis=1, keepdims=True)


def hidden_body(owners, mask, hidden, normed, factor, ids):
    inputs = hidden[...].astype(jnp.float32)
    rows = inputs.shape[0]
    center = inputs - jnp.mean(inputs, axis=-1, keepdims=True)
    inverse = lax.rsqrt(jnp.mean(center * center, axis=-1, keepdims=True) + epsilon)
    normed[...] = center * inverse
    live = token_values(mask, rows) == 1
    factor[...] = jnp.broadcast_to(jnp.where(live, inverse, 0.0), factor.shape)
    ids[...] = jnp.broadcast_to(token_values(owners, rows), ids.shape)


def owner_at(moved, groups):
    me = lax.axis_index("grp")
    place = jnp.where(lax.rem(me, 2) == 0, me // 2, groups - 1 - me // 2)
    place = lax.rem(place + moved + groups, groups)
    return jnp.where(place < groups // 2, 2 * place, 2 * (groups - 1 - place) + 1)


def slot_owners(groups):
    _, core = chip_and_core()
    sign = 2 * core - 1
    owners = [owner_at(0, groups)]
    for step in range(1, groups // 2):
        owners += [owner_at(sign * step, groups), owner_at(-sign * step, groups)]
    return owners + [owner_at(groups // 2, groups)]


def join_halves(mine, theirs, joined):
    _, core = chip_and_core()
    rows = mine.shape[0]
    joined[pl.ds(pl.multiple_of(core * rows, 16), rows), :] = mine[...]
    joined[pl.ds(pl.multiple_of((1 - core) * rows, 16), rows), :] = theirs[...]


def add_predictions(ids, normed, weights, ids_of):
    values, owner_of = normed[...].astype(jnp.bfloat16), ids[:, :1]
    total = None
    for weight, owner in zip(weights, ids_of):
        picked = jnp.where(owner_of == owner, values, jnp.zeros_like(values))
        part = lax.dot_general(
            picked, weight[...], (((1,), (1,)), ((), ())), preferred_element_type=jnp.float32
        )
        total = part if total is None else total + part
    return total


def predict_body(groups, ids, normed, *refs):
    weights, prediction = refs[:-1], refs[-1]
    prediction[...] = add_predictions(ids, normed, weights, slot_owners(groups))


def predict_more_body(groups, done, ids, normed, earlier, *refs):
    weights, prediction = refs[:-1], refs[-1]
    places = slot_owners(groups)[done : done + len(weights)]
    prediction[...] = earlier[...] + add_predictions(ids, normed, weights, places)


def predict_rest_body(groups, ids, normed, earlier, mine, theirs, *refs):
    weights, (prediction, joined) = refs[:-2], refs[-2:]
    join_halves(mine, theirs, joined)
    places = slot_owners(groups)[groups - 1 - len(weights) :]
    prediction[...] = earlier[...] + add_predictions(ids, normed, (*weights, joined), places)


def cut_body(whole, first, second):
    _, core = chip_and_core()
    rows = first.shape[0]
    first[...] = whole[pl.ds(pl.multiple_of(core * rows, 16), rows), :]
    second[...] = whole[pl.ds(pl.multiple_of((1 - core) * rows, 16), rows), :]


def join_body(first, second, joined):
    join_halves(first, second, joined)


def pick_upstream(residual, ids, weights, ids_of):
    owner_of = jnp.tile(ids[...], (1, weights[0].shape[1] // ids.shape[1]))
    total = None
    for weight, owner in zip(weights, ids_of):
        part = jnp.dot(residual, weight[...], preferred_element_type=jnp.float32)
        total = part if total is None else jnp.where(owner_of == owner, part, total)
    return total


def finish_body(groups, ids, normed, factor, attended, returned, prediction, *refs):
    weights, (targets, grad) = refs[:-2], refs[-2:]
    chip, _ = chip_and_core()
    width, _ = targets.shape
    mine, theirs = attended[...], returned[...].astype(jnp.float32)
    joined = jnp.concatenate(
        [jnp.where(chip == 0, mine, theirs), jnp.where(chip == 0, theirs, mine)], axis=1
    )
    lane = lax.broadcasted_iota(jnp.int32, joined.shape, 1) >= HEAD
    joined = jnp.where(lane, joined, 0.0)
    mean = jnp.sum(joined, axis=1, keepdims=True) * (1.0 / width)
    center = jnp.where(lane, joined - mean, 0.0)
    variance = jnp.sum(center * center, axis=1, keepdims=True) * (1.0 / width)
    found = (center * lax.rsqrt(variance + epsilon))[:, HEAD:].astype(jnp.bfloat16)
    targets[...] = found.T
    residual = (prediction[...] - found.astype(jnp.float32)).astype(jnp.bfloat16)
    upstream = pick_upstream(residual, ids, weights, slot_owners(groups))
    values = normed[...]
    mean = jnp.mean(upstream, axis=-1, keepdims=True)
    cross = jnp.mean(upstream * values, axis=-1, keepdims=True)
    scale = jnp.tile(factor[...], (1, values.shape[1] // factor.shape[1]))
    grad[...] = (scale * (upstream - mean - values * cross)).astype(grad.dtype)


def ring_pairs(members, groups):
    order = list(range(0, groups, 2)) + list(range(groups - 1, 0, -2))
    pairs = []
    for member in range(members):
        for i in range(groups):
            a, b = order[i], order[(i + 1) % groups]
            a, b = (a, b) if member % 2 == 0 else (b, a)
            pairs.append((member * groups + a, member * groups + b))
    return pairs


def paired_shards(
    tokens, target_kv, context_kv, query_weight, pred_hidden, pred_weight, target_mask, owners
):
    members = lax.axis_size("seq")
    groups = lax.axis_size("grp")
    across = [(i, (i + members // 2) % members) for i in range(members)]
    beside = [(i, i ^ 1) for i in range(members)]
    ring = ring_pairs(members, groups)
    rows, width = tokens.shape[1], query_weight.shape[0]
    features = tokens.shape[2]
    half = features // 2
    packed = 3 * LANES
    out_rows, pred_size = pred_weight.shape[1:]
    owner_row, mask_row = owners.reshape(1, -1), target_mask.reshape(1, -1)
    sums_shape = shape_of((rows, 2 * packed), jnp.float32)

    new_kv = (
        keep_rate * target_kv.astype(jnp.float32)
        + (1.0 - keep_rate) * context_kv.astype(jnp.float32)
    ).astype(jnp.bfloat16)
    normed, keep, send = local_call(
        norm_body,
        [shape_of((rows, features)), shape_of((rows, half)), shape_of((rows, half))],
        (tokens[0],),
    )
    other_kv = lax.ppermute(new_kv, "seq", beside)
    kept_other = lax.ppermute(send, "seq", across)
    joined, own_sum, q_own, own_send, stored_kv = local_call(
        first_partial_body,
        [
            shape_of((half, 2 * width)),
            sums_shape,
            shape_of((rows, packed)),
            shape_of((rows, 3 * packed)),
            shape_of(target_kv.shape),
        ],
        (new_kv, other_kv, keep, normed, query_weight),
        out_specs=[VM] * 4 + [HBM],
        scratch=[pltpu.SemaphoreType.DMA],
        cost=matmul_cost(rows, half, 4 * width),
    )
    received = lax.ppermute(own_send, "seq", across)
    other_sum, other_send = local_call(
        partial_body,
        [sums_shape, shape_of((rows, 2 * packed))],
        (kept_other, joined),
        cost=matmul_cost(rows, half, 2 * width),
    )
    from_other = lax.ppermute(other_send, "seq", across)
    kv, queries = local_call(
        kv_body,
        [shape_of((2 * rows, 2 * packed)), shape_of((2 * rows, packed))],
        (own_sum, other_sum, from_other, received, q_own),
    )
    kv_beside = lax.ppermute(kv, "seq", beside)
    attended, send_back = local_call(
        attend_body,
        [shape_of((rows, packed), jnp.float32), shape_of((rows, packed))],
        (queries, kv, kv_beside),
        cost=matmul_cost(2 * rows, 12 * LANES, 4 * rows, 12 * rows * 4 * rows),
    )
    returned = lax.ppermute(send_back, "seq", across)

    half_rows = out_rows // 2
    half_shape, whole_shape = shape_of((half_rows, pred_size)), shape_of((out_rows, pred_size))
    halves = [half_shape, half_shape]
    weights = [pred_weight[0]]
    last_step = groups // 2
    for step in range(1, last_step):
        if step == 1:
            held = lax.ppermute(pred_weight[0], ("seq", "grp"), ring)
            first, second = local_call(cut_body, halves, (held,))
        else:
            first = lax.ppermute(first, ("seq", "grp"), ring)
            second = lax.ppermute(second, ("seq", "grp"), ring)
            held = local_call(join_body, whole_shape, (first, second))
        weights += [held, lax.ppermute(held, "seq", beside)]
    if last_step == 1:
        first, second = local_call(cut_body, halves, (pred_weight[0],))
    mine = lax.ppermute(first, ("seq", "grp"), ring)
    theirs = lax.ppermute(mine, "seq", beside)
    early, most = min(3, groups - 1), groups - 1
    normed_hidden, factor, ids = local_call(
        hidden_body,
        [
            shape_of((rows, pred_size), jnp.float32),
            shape_of((rows, LANES), jnp.float32),
            shape_of((rows, LANES), jnp.int32),
        ],
        (owner_row, mask_row, pred_hidden[0]),
    )
    prediction = local_call(
        functools.partial(predict_body, groups),
        shape_of((rows, width), jnp.float32),
        (ids, normed_hidden, *weights[:early]),
        cost=matmul_cost(rows, early * pred_size, width),
    )
    if most > early:
        prediction = local_call(
            functools.partial(predict_more_body, groups, early),
            shape_of((rows, width), jnp.float32),
            (ids, normed_hidden, prediction, *weights[early:most]),
            cost=matmul_cost(rows, (most - early) * pred_size, width),
        )
    prediction, opposite = local_call(
        functools.partial(predict_rest_body, groups),
        [shape_of((rows, width), jnp.float32), whole_shape],
        (ids, normed_hidden, prediction, mine, theirs),
        cost=matmul_cost(rows, pred_size, width),
    )
    weights.append(opposite)
    targets, grad = local_call(
        functools.partial(finish_body, groups),
        [shape_of((width, rows)), shape_of((rows, pred_size))],
        (ids, normed_hidden, factor, attended, returned, prediction, *weights),
        out_specs=[pl.BlockSpec(), pl.BlockSpec()],
        cost=matmul_cost(rows, groups * pred_size, width),
    )
    return (stored_kv, targets.T[None], grad[None])


def shards(*arguments):
    pred_weight = arguments[5]
    gathered = lax.axis_size("grp") * pred_weight.size * pred_weight.dtype.itemsize
    two_chips = lax.axis_size("seq") == 4
    if two_chips and lax.axis_size("grp") % 2 == 0 and gathered <= PAIR_BUDGET:
        return paired_shards(*arguments)
    return general_shards(*arguments)


def solution(mesh):
    placed = (
        P("grp", "seq", None),
        P("seq", None),
        P("seq", None),
        P(),
        P("grp", "seq", None),
        P("grp", None, None),
        P("grp", "seq"),
        P("grp", "seq", None),
    )
    return jax.shard_map(
        shards,
        mesh=mesh,
        in_specs=placed,
        out_specs=(P("seq", None), P("grp", "seq", None), P("grp", "seq", None)),
        check_vma=False,
    )
```

```python
import functools
import math

import jax
import jax.numpy as jnp
from jax import lax
from jax.experimental import pallas as pl
from jax.experimental.pallas import tpu as pltpu
from jax.sharding import PartitionSpec as P


HEAD = 64
HEADS = 11


keep_rate = 0.9
epsilon = 1e-05


def layer_norm(values):
    center = values - jnp.mean(values, axis=-1, keepdims=True)
    variance = jnp.mean(center * center, axis=-1, keepdims=True)
    return center * lax.rsqrt(variance + epsilon)


def norm_backward(upstream, normed, inputs):
    center = inputs - jnp.mean(inputs, axis=-1, keepdims=True)
    variance = jnp.mean(center * center, axis=-1, keepdims=True)
    inverse = lax.rsqrt(variance + epsilon)
    upstream_mean = jnp.mean(upstream, axis=-1, keepdims=True)
    cross_mean = jnp.mean(upstream * normed, axis=-1, keepdims=True)
    return inverse * (upstream - upstream_mean - normed * cross_mean)


def owner_compute(received, expert_weight):
    received_targets, received_hidden = received
    groups = received_targets.shape[0]
    items = received_targets.shape[1]
    pred_size = expert_weight.shape[1]
    width = expert_weight.shape[0]
    inputs = received_hidden.reshape(-1, pred_size).astype(jnp.float32)
    normed = layer_norm(inputs)
    prediction = jnp.einsum(
        "tp,ap->ta", normed.astype(jnp.bfloat16), expert_weight, preferred_element_type=jnp.float32
    )
    residual = prediction - received_targets.reshape(-1, width).astype(jnp.float32)
    upstream = jnp.dot(
        residual.astype(jnp.bfloat16), expert_weight, preferred_element_type=jnp.float32
    )
    grad = norm_backward(upstream, normed, inputs).astype(jnp.bfloat16)
    return grad.reshape(groups, items, 2 * pred_size)


def general_shards(
    tokens, target_kv, context_kv, query_weight, pred_hidden, pred_weight, target_mask, owners
):
    new_kv = (
        keep_rate * target_kv.astype(jnp.float32)
        + (1.0 - keep_rate) * context_kv.astype(jnp.float32)
    ).astype(jnp.bfloat16)
    width = HEADS * HEAD
    scale = 1.0 / math.sqrt(HEAD)
    rows = tokens.shape[1]
    normed = layer_norm(tokens[0].astype(jnp.float32)).astype(jnp.bfloat16)
    queries = jnp.einsum(
        "td,ad->ta", normed, query_weight, preferred_element_type=jnp.float32
    ).astype(jnp.bfloat16)
    query_heads = queries.reshape(rows, HEADS, HEAD)
    own_kv = jnp.dot(
        normed,
        lax.all_gather(new_kv, "seq", axis=0, tiled=True),
        preferred_element_type=jnp.float32,
    ).astype(jnp.bfloat16)
    key_values = lax.all_gather(own_kv, "seq", axis=0, tiled=True)
    count = key_values.shape[0]
    keys = key_values[:, :width].reshape(count, HEADS, HEAD)
    values = key_values[:, width:].reshape(count, HEADS, HEAD)
    scores = (
        jnp.einsum("qhd,khd->hqk", query_heads, keys, preferred_element_type=jnp.float32) * scale
    )
    expo = jnp.exp(scores)
    added = jnp.einsum(
        "hqk,khd->qhd", expo.astype(jnp.bfloat16), values, preferred_element_type=jnp.float32
    )
    numerator = added.reshape(rows, width)
    denominator = jnp.sum(expo, axis=-1)
    attended = (numerator.reshape(rows, HEADS, HEAD) / denominator.T[:, :, None]).reshape(
        rows, width
    )
    targets = layer_norm(attended).astype(jnp.bfloat16)
    blocks = target_mask.shape[1]
    groups = lax.axis_size("grp")
    capacity = max(2, (blocks + groups - 1) // groups)
    pred_size = pred_hidden.shape[2]
    owner_ids = owners[0, :, 0]
    live = target_mask[0]
    chosen = (
        (owner_ids[:, None] == jnp.arange(groups, dtype=jnp.int32)[None, :]) & (live[:, None] == 1)
    ).astype(jnp.int32)
    earlier = jnp.cumsum(chosen, axis=0) - chosen
    position = jnp.sum(earlier * chosen, axis=1)
    slot_index = owner_ids * capacity + position
    dispatch = (
        (jnp.arange(groups * capacity, dtype=jnp.int32)[:, None] == slot_index[None, :])
        & (live[None, :] == 1)
    ).astype(jnp.bfloat16)
    send_targets = (
        jnp.dot(dispatch, targets.reshape(blocks, 2 * width), preferred_element_type=jnp.float32)
        .astype(jnp.bfloat16)
        .reshape(groups, capacity, 2 * width)
    )
    send_hidden = (
        jnp.dot(
            dispatch,
            pred_hidden[0].reshape(blocks, 2 * pred_size),
            preferred_element_type=jnp.float32,
        )
        .astype(jnp.bfloat16)
        .reshape(groups, capacity, 2 * pred_size)
    )
    expert_weight = pred_weight[0]
    owner_grads = owner_compute(
        (
            lax.all_to_all(send_targets, "grp", split_axis=0, concat_axis=0, tiled=True),
            lax.all_to_all(send_hidden, "grp", split_axis=0, concat_axis=0, tiled=True),
        ),
        expert_weight,
    )
    back_grads = lax.all_to_all(owner_grads, "grp", split_axis=0, concat_axis=0, tiled=True)
    pair_grads = jnp.dot(
        dispatch.T,
        back_grads.reshape(groups * capacity, 2 * pred_size),
        preferred_element_type=jnp.float32,
    )
    pred_grad = pair_grads.astype(jnp.bfloat16).reshape(rows, pred_size)
    return (new_kv, targets[None], pred_grad[None])


LANES = 128
PAIR_BUDGET = 16 << 20
VM = pl.BlockSpec(memory_space=pltpu.VMEM)
HBM = pl.BlockSpec(memory_space=pltpu.HBM)


def local_call(body, outs, operands, specs=None, out_specs=None, cost=None, scratch=(), limit=4):
    return pl.pallas_call(
        body,
        out_shape=outs,
        in_specs=specs or [VM] * len(operands),
        out_specs=out_specs or jax.tree.map(lambda _: VM, outs),
        scratch_shapes=list(scratch),
        cost_estimate=cost,
        compiler_params=pltpu.CompilerParams(vmem_limit_bytes=limit << 20),
    )(*operands)


def shape_of(dims, kind=jnp.bfloat16):
    return jax.ShapeDtypeStruct(dims, kind)


def matmul_cost(rows, depth, columns, extra=0):
    return pl.CostEstimate(
        flops=2 * rows * depth * columns, bytes_accessed=2 * depth * columns, transcendentals=extra
    )


def chip_and_core():
    me = lax.axis_index("seq")
    return me // 2, lax.rem(me, 2)


def chip_tiles(tiles, is_first, with_values):
    lane = lax.broadcasted_iota(jnp.int32, tiles[0].shape, 1) < HEAD
    mixed = jnp.where(lane, tiles[5], tiles[2])
    first = [tiles[0], tiles[1], tiles[2]]
    second = [tiles[3], tiles[4], mixed]
    if with_values:
        first = first + tiles[5:8]
        second = second + tiles[8:11]
    own = [jnp.where(is_first, a, b) for a, b in zip(first, second)]
    other = [jnp.where(is_first, b, a) for a, b in zip(first, second)]
    return own, other


def norm_body(tokens, normed, keep, send):
    half = tokens.shape[1] // 2
    chip, _ = chip_and_core()
    values = layer_norm(tokens[...].astype(jnp.float32)).astype(jnp.bfloat16)
    normed[...] = values
    low, high = values[:, :half], values[:, half:]
    keep[...] = jnp.where(chip == 0, low, high)
    send[...] = jnp.where(chip == 0, high, low)


def split_product(rows, weight, own, other):
    chip, _ = chip_and_core()
    sums = jnp.dot(rows[...], weight[...], preferred_element_type=jnp.float32)
    tiles = [sums[:, t * LANES : (t + 1) * LANES] for t in range(sums.shape[1] // LANES)]
    mine, theirs = chip_tiles(tiles, chip == 0, True)
    for t in range(6):
        own[:, t * LANES : (t + 1) * LANES] = mine[t]
        other[:, t * LANES : (t + 1) * LANES] = theirs[t].astype(jnp.bfloat16)


def blend(target, context):
    return (
        keep_rate * target[...].astype(jnp.float32)
        + (1.0 - keep_rate) * context[...].astype(jnp.float32)
    ).astype(jnp.bfloat16)


def first_partial_body(
    target, context, other_target, other_context, rows, normed, query_weight,
    joined, own, q_own, send, stored, sem,
):
    chip, core = chip_and_core()
    depth = target.shape[0]
    own_rows = pl.ds(pl.multiple_of(core * depth, 16), depth)
    joined[own_rows, :] = blend(target, context)
    store = pltpu.make_async_copy(joined.at[own_rows], stored, sem)
    store.start()
    joined[pl.ds(pl.multiple_of((1 - core) * depth, 16), depth), :] = blend(
        other_target, other_context
    )
    split_product(rows, joined, own, send)
    queries = lax.dot_general(
        normed[...], query_weight[...], (((1,), (1,)), ((), ())), preferred_element_type=jnp.float32
    ).astype(jnp.bfloat16).astype(jnp.float32) * (1.0 / math.sqrt(HEAD))
    full = queries.shape[1] // LANES
    tiles = [queries[:, t * LANES : (t + 1) * LANES] for t in range(full)]
    rest = queries[:, full * LANES :]
    tiles.append(jnp.concatenate([rest, jnp.zeros_like(rest)], axis=1))
    mine, theirs = chip_tiles(tiles, chip == 0, False)
    for t in range(3):
        q_own[:, t * LANES : (t + 1) * LANES] = mine[t].astype(jnp.bfloat16)
        send[:, (6 + t) * LANES : (7 + t) * LANES] = theirs[t].astype(jnp.bfloat16)
    store.wait()


def partial_body(rows, weight, own, other):
    split_product(rows, weight, own, other)


def kv_body(own_sum, other_sum, from_other, received, q_own, kv, queries):
    rows, width = own_sum.shape
    kv[:rows, :] = (other_sum[...] + received[:, :width].astype(jnp.float32)).astype(kv.dtype)
    kv[rows:, :] = (own_sum[...] + from_other[...].astype(jnp.float32)).astype(kv.dtype)
    queries[:rows, :] = q_own[...]
    queries[rows:, :] = received[:, width:]


def add_keys(queries, kv_refs, slot):
    upper_lane = lax.broadcasted_iota(jnp.int32, (1, LANES), 1) >= HEAD
    tile, upper = slot // 2, slot % 2
    lane = upper_lane if upper else jnp.logical_not(upper_lane)
    q = queries[:, tile * LANES : (tile + 1) * LANES]
    q = jnp.where(lane, q, jnp.zeros_like(q))
    v_tile, v_upper = (slot + 1) % 6 // 2, (slot + 1) % 2
    v_lane = upper_lane if v_upper else jnp.logical_not(upper_lane)
    total = None
    for kv in kv_refs:
        keys = kv[:, tile * LANES : (tile + 1) * LANES]
        scores = lax.dot_general(
            q, keys, (((1,), (1,)), ((), ())), preferred_element_type=jnp.float32
        )
        weights = jnp.exp(scores).astype(jnp.bfloat16)
        start = (3 + v_tile) * LANES
        values = kv[:, start : start + LANES]
        values = jnp.where(v_lane, values, jnp.ones_like(values))
        part = jnp.dot(weights, values, preferred_element_type=jnp.float32)
        total = part if total is None else total + part
    return total


def attend_body(queries, kv_a, kv_b, mine, theirs, last):
    chip, _ = chip_and_core()
    upper_lane = lax.broadcasted_iota(jnp.int32, (1, LANES), 1) >= HEAD
    rows = mine.shape[0]
    found = [None] * 6

    @pl.when(chip == 0)
    def _():
        last[...] = jnp.zeros_like(last)

    @pl.when(chip != 0)
    def _():
        total = add_keys(queries, (kv_a, kv_b), 5)
        last[...] = total / pltpu.roll(total, HEAD, 1)

    for slot in range(5):
        total = add_keys(queries, (kv_a, kv_b), slot)
        found[slot + 1] = total / pltpu.roll(total, HEAD, 1)
    found[0] = last[...]
    for t in range(3):
        joined = jnp.where(upper_lane, found[2 * t + 1], found[2 * t])
        mine[:, t * LANES : (t + 1) * LANES] = joined[:rows]
        theirs[:, t * LANES : (t + 1) * LANES] = joined[rows:].astype(theirs.dtype)


def token_values(pairs, rows):
    shape = (rows, pairs.shape[1])
    token = lax.broadcasted_iota(jnp.int32, shape, 0) // 2
    pair = lax.broadcasted_iota(jnp.int32, shape, 1)
    return jnp.sum(jnp.where(token == pair, pairs[...], 0), axis=1, keepdims=True)


def hidden_body(owners, mask, hidden, normed, factor, ids):
    inputs = hidden[...].astype(jnp.float32)
    rows = inputs.shape[0]
    center = inputs - jnp.mean(inputs, axis=-1, keepdims=True)
    inverse = lax.rsqrt(jnp.mean(center * center, axis=-1, keepdims=True) + epsilon)
    normed[...] = center * inverse
    live = token_values(mask, rows) == 1
    factor[...] = jnp.broadcast_to(jnp.where(live, inverse, 0.0), factor.shape)
    ids[...] = jnp.broadcast_to(token_values(owners, rows), ids.shape)


def owner_at(moved, groups):
    me = lax.axis_index("grp")
    place = jnp.where(lax.rem(me, 2) == 0, me // 2, groups - 1 - me // 2)
    place = lax.rem(place + moved + groups, groups)
    return jnp.where(place < groups // 2, 2 * place, 2 * (groups - 1 - place) + 1)


def slot_owners(groups):
    _, core = chip_and_core()
    sign = 1 - 2 * core
    owners = [owner_at(0, groups)]
    for step in range(1, groups // 2):
        owners += [owner_at(sign * step, groups), owner_at(-sign * step, groups)]
    return owners + [owner_at(groups // 2, groups)]


def join_halves(mine, theirs, joined):
    _, core = chip_and_core()
    rows = mine.shape[0]
    joined[pl.ds(pl.multiple_of(core * rows, 16), rows), :] = mine[...]
    joined[pl.ds(pl.multiple_of((1 - core) * rows, 16), rows), :] = theirs[...]


def add_predictions(ids, normed, weights, ids_of):
    values, owner_of = normed[...].astype(jnp.bfloat16), ids[:, :1]
    total = None
    for weight, owner in zip(weights, ids_of):
        picked = jnp.where(owner_of == owner, values, jnp.zeros_like(values))
        part = lax.dot_general(
            picked, weight[...], (((1,), (1,)), ((), ())), preferred_element_type=jnp.float32
        )
        total = part if total is None else total + part
    return total


def predict_body(groups, ids, normed, *refs):
    weights, prediction = refs[:-1], refs[-1]
    prediction[...] = add_predictions(ids, normed, weights, slot_owners(groups))


def predict_more_body(groups, done, ids, normed, earlier, *refs):
    weights, prediction = refs[:-1], refs[-1]
    places = slot_owners(groups)[done : done + len(weights)]
    prediction[...] = earlier[...] + add_predictions(ids, normed, weights, places)


def predict_rest_body(groups, ids, normed, earlier, mine, theirs, *refs):
    weights, (prediction, joined) = refs[:-2], refs[-2:]
    join_halves(mine, theirs, joined)
    places = slot_owners(groups)[groups - 1 - len(weights) :]
    prediction[...] = earlier[...] + add_predictions(ids, normed, (*weights, joined), places)


def cut_body(whole, first, second):
    _, core = chip_and_core()
    rows = first.shape[0]
    first[...] = whole[pl.ds(pl.multiple_of(core * rows, 16), rows), :]
    second[...] = whole[pl.ds(pl.multiple_of((1 - core) * rows, 16), rows), :]


def join_body(first, second, joined):
    join_halves(first, second, joined)


def pick_upstream(residual, ids, weights, ids_of):
    owner_of = jnp.tile(ids[...], (1, weights[0].shape[1] // ids.shape[1]))
    total = None
    for weight, owner in zip(weights, ids_of):
        part = jnp.dot(residual, weight[...], preferred_element_type=jnp.float32)
        total = part if total is None else jnp.where(owner_of == owner, part, total)
    return total


def finish_body(groups, ids, normed, factor, attended, returned, prediction, *refs):
    weights, (targets, grad) = refs[:-2], refs[-2:]
    chip, _ = chip_and_core()
    width, _ = targets.shape
    mine, theirs = attended[...], returned[...].astype(jnp.float32)
    joined = jnp.concatenate(
        [jnp.where(chip == 0, mine, theirs), jnp.where(chip == 0, theirs, mine)], axis=1
    )
    lane = lax.broadcasted_iota(jnp.int32, joined.shape, 1) >= HEAD
    joined = jnp.where(lane, joined, 0.0)
    mean = jnp.sum(joined, axis=1, keepdims=True) * (1.0 / width)
    center = jnp.where(lane, joined - mean, 0.0)
    variance = jnp.sum(center * center, axis=1, keepdims=True) * (1.0 / width)
    found = (center * lax.rsqrt(variance + epsilon))[:, HEAD:].astype(jnp.bfloat16)
    targets[...] = found.T
    residual = (prediction[...] - found.astype(jnp.float32)).astype(jnp.bfloat16)
    upstream = pick_upstream(residual, ids, weights, slot_owners(groups))
    values = normed[...]
    mean = jnp.mean(upstream, axis=-1, keepdims=True)
    cross = jnp.mean(upstream * values, axis=-1, keepdims=True)
    scale = jnp.tile(factor[...], (1, values.shape[1] // factor.shape[1]))
    grad[...] = (scale * (upstream - mean - values * cross)).astype(grad.dtype)


def ring_pairs(members, groups):
    order = list(range(0, groups, 2)) + list(range(groups - 1, 0, -2))
    pairs = []
    for member in range(members):
        for i in range(groups):
            a, b = order[i], order[(i + 1) % groups]
            a, b = (b, a) if member % 2 == 0 else (a, b)
            pairs.append((member * groups + a, member * groups + b))
    return pairs


def paired_shards(
    tokens, target_kv, context_kv, query_weight, pred_hidden, pred_weight, target_mask, owners
):
    members = lax.axis_size("seq")
    groups = lax.axis_size("grp")
    across = [(i, (i + members // 2) % members) for i in range(members)]
    beside = [(i, i ^ 1) for i in range(members)]
    ring = ring_pairs(members, groups)
    rows, width = tokens.shape[1], query_weight.shape[0]
    features = tokens.shape[2]
    half = features // 2
    packed = 3 * LANES
    out_rows, pred_size = pred_weight.shape[1:]
    owner_row, mask_row = owners.reshape(1, -1), target_mask.reshape(1, -1)
    sums_shape = shape_of((rows, 2 * packed), jnp.float32)

    other_target = lax.ppermute(target_kv, "seq", beside)
    other_context = lax.ppermute(context_kv, "seq", beside)
    normed, keep, send = local_call(
        norm_body,
        [shape_of((rows, features)), shape_of((rows, half)), shape_of((rows, half))],
        (tokens[0],),
        cost=pl.CostEstimate(flops=1 << 33, bytes_accessed=1 << 20, transcendentals=0),
    )
    kept_other = lax.ppermute(send, "seq", across)
    joined, own_sum, q_own, own_send, stored_kv = local_call(
        first_partial_body,
        [
            shape_of((half, 2 * width)),
            sums_shape,
            shape_of((rows, packed)),
            shape_of((rows, 3 * packed)),
            shape_of(target_kv.shape),
        ],
        (target_kv, context_kv, other_target, other_context, keep, normed, query_weight),
        out_specs=[VM] * 4 + [HBM],
        scratch=[pltpu.SemaphoreType.DMA],
        cost=matmul_cost(rows, half, 4 * width),
    )
    received = lax.ppermute(own_send, "seq", across)
    other_sum, other_send = local_call(
        partial_body,
        [sums_shape, shape_of((rows, 2 * packed))],
        (kept_other, joined),
        cost=matmul_cost(rows, half, 2 * width),
    )
    from_other = lax.ppermute(other_send, "seq", across)
    kv, queries = local_call(
        kv_body,
        [shape_of((2 * rows, 2 * packed)), shape_of((2 * rows, packed))],
        (own_sum, other_sum, from_other, received, q_own),
    )
    kv_beside = lax.ppermute(kv, "seq", beside)
    attended, send_back = local_call(
        attend_body,
        [shape_of((rows, packed), jnp.float32), shape_of((rows, packed))],
        (queries, kv, kv_beside),
        scratch=[pltpu.VMEM((2 * rows, LANES), jnp.float32)],
        cost=matmul_cost(2 * rows, 12 * LANES, 4 * rows, 12 * rows * 4 * rows),
    )
    returned = lax.ppermute(send_back, "seq", across)

    half_rows = out_rows // 2
    half_shape, whole_shape = shape_of((half_rows, pred_size)), shape_of((out_rows, pred_size))
    halves = [half_shape, half_shape]
    weights = [pred_weight[0]]
    last_step = groups // 2
    for step in range(1, last_step):
        if step == 1:
            held = lax.ppermute(pred_weight[0], ("seq", "grp"), ring)
            first, second = local_call(cut_body, halves, (held,))
        else:
            first = lax.ppermute(first, ("seq", "grp"), ring)
            second = lax.ppermute(second, ("seq", "grp"), ring)
            held = local_call(join_body, whole_shape, (first, second))
        weights += [held, lax.ppermute(held, "seq", beside)]
    if last_step == 1:
        first, second = local_call(cut_body, halves, (pred_weight[0],))
    mine = lax.ppermute(first, ("seq", "grp"), ring)
    theirs = lax.ppermute(mine, "seq", beside)
    early, most = min(3, groups - 1), groups - 1
    normed_hidden, factor, ids = local_call(
        hidden_body,
        [
            shape_of((rows, pred_size), jnp.float32),
            shape_of((rows, LANES), jnp.float32),
            shape_of((rows, LANES), jnp.int32),
        ],
        (owner_row, mask_row, pred_hidden[0]),
    )
    prediction = local_call(
        functools.partial(predict_body, groups),
        shape_of((rows, width), jnp.float32),
        (ids, normed_hidden, *weights[:early]),
        cost=matmul_cost(rows, early * pred_size, width),
    )
    if most > early:
        prediction = local_call(
            functools.partial(predict_more_body, groups, early),
            shape_of((rows, width), jnp.float32),
            (ids, normed_hidden, prediction, *weights[early:most]),
            cost=matmul_cost(rows, (most - early) * pred_size, width),
        )
    prediction, opposite = local_call(
        functools.partial(predict_rest_body, groups),
        [shape_of((rows, width), jnp.float32), whole_shape],
        (ids, normed_hidden, prediction, mine, theirs),
        cost=matmul_cost(rows, pred_size, width),
    )
    weights.append(opposite)
    targets, grad = local_call(
        functools.partial(finish_body, groups),
        [shape_of((width, rows)), shape_of((rows, pred_size))],
        (ids, normed_hidden, factor, attended, returned, prediction, *weights),
        out_specs=[pl.BlockSpec(), pl.BlockSpec()],
        cost=matmul_cost(rows, groups * pred_size, width),
    )
    return (stored_kv, targets.T[None], grad[None])


def shards(*arguments):
    pred_weight = arguments[5]
    gathered = lax.axis_size("grp") * pred_weight.size * pred_weight.dtype.itemsize
    two_chips = lax.axis_size("seq") == 4
    if two_chips and lax.axis_size("grp") % 2 == 0 and gathered <= PAIR_BUDGET:
        return paired_shards(*arguments)
    return general_shards(*arguments)


def solution(mesh):
    placed = (
        P("grp", "seq", None),
        P("seq", None),
        P("seq", None),
        P(),
        P("grp", "seq", None),
        P("grp", None, None),
        P("grp", "seq"),
        P("grp", "seq", None),
    )
    return jax.shard_map(
        shards,
        mesh=mesh,
        in_specs=placed,
        out_specs=(P("seq", None), P("grp", "seq", None), P("grp", "seq", None)),
        check_vma=False,
    )
```
